128 devices in a mesh: ctx: 16 (over z, x), head: 8 (over y, core).
Axes of the slice: x: 4, y: 4, z: 4, core: 2. Of those that a mesh axis runs over, the one named last changes fastest.
Arguments:
- values: bfloat16 [16384, 5120], P(('ctx', 'head')), may hold values from -6 to 6
- state_in: bfloat16 [16384, 128], P('ctx'), may hold values from -0.5 to 0.5
- state_out: bfloat16 [16384, 128], P('ctx'), may hold values from -6 to 6
- log_decay: float32 [16384, 80], P('ctx', 'head'), may hold values from -1 to 0
- level_class: int32 [16384], P('ctx'), may hold values from 0 to 31
- level_table: float32 [32, 9, 80], P(None, None, 'head'), may hold values from 0.2 to 2
- skip_gain: float32 [80], P('head'), may hold values from 0.5 to 2
- norm_gain: float32 [5120], P('head'), may hold values from 0.1 to 1.9
- out_weight: bfloat16 [5120, 2560], P('head', 'ctx'), may hold values from -0.078125 to 0.078125
Outputs:
- projected: bfloat16 [16384, 2560], P(('ctx', 'head'))
The draws below stay inside these ranges and needn't reach their ends.
All inputs are finite; a program needn't handle non-finite values.
Results may differ from the reference program's by a relative error of at most 0.0049.
Values may be sent and summed in bfloat16 or wider, within the bound.
A program may use at most 128 MiB of HBM per device.

```python
import math
import jax
import jax.numpy as jnp
from jax import lax

D = 2560
HEADS = 80
P_SIZE = 64
N_STATE = 128
CH = 64
CLASSES = 32
STRETCHES_DEV = 16
TOK_DEV = 1024
SEQUENCE_TOKENS = 16384
D_INNER = 5120
LEVELS = 9


def draw_log_decay(key, part):
    split_random_keys = jax.random.split(key, 7)
    picked = jax.random.uniform(split_random_keys[0], (HEADS,))
    fast_share = 0.5
    rough_low = 0.5
    rough_high = 1.5
    fast_head = picked < fast_share
    fast_rate = jnp.exp(jax.random.uniform(split_random_keys[1], (HEADS,), minval=jnp.log(1.0 / 50.0), maxval=jnp.log(1.0 / 30.0)))
    slow_total = jnp.exp(jax.random.uniform(split_random_keys[2], (HEADS,), minval=jnp.log(0.05), maxval=jnp.log(0.3)))
    baseline_rate = jnp.where(fast_head, fast_rate, slow_total / SEQUENCE_TOKENS)
    partition_factor = jnp.exp(jax.random.uniform(split_random_keys[3], (SEQUENCE_TOKENS // TOK_DEV, HEADS), minval=jnp.log(0.5), maxval=jnp.log(2.0)))
    partition_factor = jnp.repeat(partition_factor, TOK_DEV, axis=0)
    coarseness_level = jax.random.uniform(split_random_keys[4], (SEQUENCE_TOKENS, HEADS), minval=rough_low, maxval=rough_high)
    surge_position = jax.random.randint(split_random_keys[5], (2,), 0, SEQUENCE_TOKENS)
    surge_length = jax.random.uniform(split_random_keys[6], (2,), minval=0.22, maxval=0.69)
    surge_struck = jnp.arange(SEQUENCE_TOKENS)[:, None] == surge_position[None, :]
    surge_penalty = jnp.sum(jnp.where(surge_struck, surge_length[None, :], 0.0), axis=1)
    return -(baseline_rate[None, :] * partition_factor * coarseness_level + surge_penalty[:, None])


def place_ends(entries, key, least, top_value):
    shape = entries.shape
    index_at = [jax.random.randint(jax.random.fold_in(key, axis), (), 0, shape[axis]) for axis in range(len(shape))]
    entries = entries.at[tuple(index_at)].set(least)
    longest = shape.index(max(shape))
    index_at[longest] = (index_at[longest] + 1) % shape[longest]
    return entries.at[tuple(index_at)].set(top_value)


def block_levels(own_key, extent, cuts, low, high):
    def one(position, blocks):
        steps = jax.random.uniform(jax.random.fold_in(jax.random.fold_in(own_key, 6), position), (blocks,), jnp.float32, low / len(cuts), high / len(cuts))
        return jnp.repeat(jnp.exp(steps), extent[position] // blocks).reshape((-1,) + (1,) * (len(extent) - position - 1))

    loudness = one(*cuts[0])
    for cut in cuts[1:]:
        loudness = loudness * one(*cut)
    return loudness


def normal_values(stream_key, extent, scale, limit, cuts=(), kind=jnp.bfloat16):
    array = jax.random.normal(stream_key, extent, jnp.float32) * scale
    if len(cuts) > 0:
        array = block_levels(stream_key, extent, cuts, -0.22, 0.18) * array
    return jnp.clip(array, min=-limit, max=limit).astype(kind)


def setup_inputs(seed: int = 0) -> dict:
    key_of = jax.random.split(jax.random.key(seed), 10)
    return {
        "values": normal_values(key_of[0], (SEQUENCE_TOKENS, D_INNER), 1.0, 6.0, ((0, 128),)),
        "state_in": normal_values(key_of[1], (SEQUENCE_TOKENS, N_STATE), (N_STATE ** -0.5), 0.5, ((0, 16),)),
        "state_out": normal_values(key_of[2], (SEQUENCE_TOKENS, N_STATE), 1.0, 6.0, ((0, 16),)),
        "log_decay": draw_log_decay(jax.random.fold_in(key_of[9], 71), 0),
        "level_class": place_ends(jax.random.randint(key_of[4], (SEQUENCE_TOKENS,), 0, CLASSES), jax.random.fold_in(key_of[4], 1), 0, CLASSES - 1).astype(jnp.int32),
        "level_table": jnp.clip(jnp.exp(math.log(2.0) - 2.3025851 * jax.random.uniform(key_of[5], (CLASSES, LEVELS, HEADS), jnp.float32) ** block_levels(key_of[5], (CLASSES, LEVELS, HEADS), ((2, 8),), -0.2, 0.2)), 0.2, 2.0),
        "skip_gain": jnp.clip(0.5 + 1.5 * jax.random.uniform(key_of[6], (HEADS,), jnp.float32) ** block_levels(key_of[6], (HEADS,), ((0, 8),), -0.2, 0.2), 0.5, 2.0),
        "norm_gain": jnp.clip(1.0 + 0.18 * jax.random.normal(key_of[7], (D_INNER,), jnp.float32), 0.1, 1.9),
        "out_weight": normal_values(key_of[8], (D_INNER, D), D_INNER ** -0.5, 0.078125, ((0, 8), (1, 16))),
    }


PRECISE = lax.Precision.HIGHEST
EPSILON = 1e-05

def expand_heads(factor, head_width):
    return jnp.repeat(factor, head_width, axis=-1)

def local_levels(inputs, state_in, state_out, log_decay, weights, stretch_size, head_width, readout):
    tokens_dev = inputs.shape[0]
    features = inputs.shape[1]
    state_size = state_in.shape[1]
    head_count = log_decay.shape[1]
    stretch_count = tokens_dev // stretch_size
    height_count = stretch_count.bit_length() - 1
    within = jnp.cumsum(log_decay.reshape(stretch_count, stretch_size, head_count), axis=1)
    stretch_sum = within[:, -1]
    block_end = jnp.cumsum(stretch_sum, axis=0)
    cumul = (block_end - stretch_sum)[:, None, :] + within
    flat_cumul = cumul.reshape(tokens_dev, head_count)
    in_pieces = state_in.reshape(stretch_count, stretch_size, state_size)
    input_pieces = inputs.reshape(stretch_count, stretch_size, features)
    to_end = expand_heads(jnp.exp(stretch_sum[:, None, :] - within), head_width) * input_pieces
    merged = jnp.einsum('csn,csf->cnf', in_pieces, to_end, precision=PRECISE)
    output = None
    if readout:
        out_pieces = state_out.reshape(stretch_count, stretch_size, state_size)
        scores = jnp.einsum('ctn,csn->cts', out_pieces, in_pieces, precision=PRECISE)
        causal = jnp.arange(stretch_size)[:, None] >= jnp.arange(stretch_size)[None, :]
        scores = jnp.where(causal[None], scores, 0.0)
        lifted = expand_heads(jnp.exp(-within), head_width) * input_pieces
        direct = jnp.einsum('cts,csf->ctf', scores, lifted, precision=PRECISE)
        level_zero = weights[:, 0].reshape(stretch_count, stretch_size, head_count)
        output = (expand_heads(jnp.exp(within) * level_zero, head_width) * direct).reshape(tokens_dev, features)
    for height in range(1, height_count + 1):
        group_count = merged.shape[0] // 2
        paired = merged.reshape(group_count, 2, state_size, features)
        end_pair = block_end.reshape(group_count, 2, head_count)
        if readout:
            half_rows = tokens_dev // group_count // 2
            reader = state_out.reshape(group_count, 2, half_rows, state_size)[:, 1]
            upper_cumul = flat_cumul.reshape(group_count, 2, half_rows, head_count)[:, 1]
            upper_weight = weights[:, height].reshape(group_count, 2, half_rows, head_count)[:, 1]
            fading = jnp.exp(upper_cumul - end_pair[:, 0][:, None, :])
            gained = expand_heads(fading * upper_weight, head_width) * jnp.einsum('grn,gnf->grf', reader, paired[:, 0], precision=PRECISE)
            padded = jnp.stack([jnp.zeros_like(gained), gained], axis=1)
            output = output + padded.reshape(tokens_dev, features)
        carried = expand_heads(jnp.exp(end_pair[:, 1] - end_pair[:, 0]), head_width)
        merged = carried[:, None, :] * paired[:, 0] + paired[:, 1]
        block_end = end_pair[:, 1]
    return (output, merged[0], block_end[0], flat_cumul)

def cross_levels(output, state_out, flat_cumul, weights, every_state, every_total, block_index, local_bits, head_width):
    device_count = every_total.shape[0]
    device = jnp.arange(device_count, dtype=jnp.int32)
    between = (device[:, None] < device[None, :]) & (device[None, :] < block_index)
    span_decay = jnp.dot(between.astype(jnp.float32), every_total, precision=PRECISE)
    for bit_index in range(device_count.bit_length() - 1):
        stride = 2 ** (bit_index + 1)
        half_stride = 2 ** bit_index
        member = (device // stride == block_index // stride) & (device // half_stride % 2 == 0) & (block_index // half_stride % 2 == 1)
        factor = jnp.where(member[:, None], jnp.exp(jnp.where(member[:, None], span_decay, 0.0)), 0.0)
        bucket = jnp.einsum('df,dnf->nf', expand_heads(factor, head_width), every_state, precision=PRECISE)
        scaling = expand_heads(jnp.exp(flat_cumul) * weights[:, local_bits + 1 + bit_index], head_width)
        output = output + scaling * jnp.dot(state_out, bucket, precision=PRECISE)
    return output

def finish(output, inputs, skip_gain, norm_gain, head_width):
    output = output + expand_heads(skip_gain, head_width)[None, :] * inputs
    grouped = output.reshape(output.shape[0], -1, head_width)
    mean_square = lax.optimization_barrier(jnp.mean(grouped * grouped, axis=-1, keepdims=True))
    normed = grouped * lax.rsqrt(mean_square + EPSILON)
    return (normed.reshape(output.shape) * norm_gain[None, :]).astype(jnp.bfloat16)

def reference(values, state_in, state_out, log_decay, level_class, level_table, skip_gain, norm_gain, out_weight):
    blocks = SEQUENCE_TOKENS // TOK_DEV
    local_bits = STRETCHES_DEV.bit_length() - 1

    def block_rows(source, block_index):
        return lax.dynamic_slice_in_dim(source, (block_index * TOK_DEV).astype(jnp.int32), TOK_DEV, 0)

    def first_pass(block_index):
        outcome = local_levels(block_rows(values, block_index).astype(jnp.float32), block_rows(state_in, block_index).astype(jnp.float32), None, block_rows(log_decay, block_index), None, CH, P_SIZE, False)
        return (outcome[1], outcome[2])
    every_state, every_total = lax.map(first_pass, jnp.arange(blocks, dtype=jnp.int32))

    def second_pass(block_index):
        inputs = block_rows(values, block_index).astype(jnp.float32)
        readers = block_rows(state_out, block_index).astype(jnp.float32)
        weights = level_table[block_rows(level_class, block_index)]
        output, unused_state, unused_total, flat_cumul = local_levels(inputs, block_rows(state_in, block_index).astype(jnp.float32), readers, block_rows(log_decay, block_index), weights, CH, P_SIZE, True)
        output = cross_levels(output, readers, flat_cumul, weights, every_state, every_total, block_index, local_bits, P_SIZE)
        normed = finish(output, inputs, skip_gain, norm_gain, P_SIZE)
        return jnp.dot(normed, out_weight, preferred_element_type=jnp.float32).astype(jnp.bfloat16)
    projected = lax.map(second_pass, jnp.arange(blocks, dtype=jnp.int32))
    return projected.reshape(SEQUENCE_TOKENS, D)
```

```python
import jax
import jax.numpy as jnp
from jax import lax
from jax.experimental import pallas as pl
from jax.experimental.pallas import tpu as pltpu
from jax.sharding import PartitionSpec as P

MESH = pl.DeviceIdType.MESH
PRECISE = lax.Precision.HIGHEST
EPSILON = 1e-05
F32 = jnp.float32
BF16 = jnp.bfloat16
LANES = 128
HEADS_DEV = 10
WIDTH = 64
FEATS = HEADS_DEV * WIDTH
STATE = 128
CHUNK = 128
CHUNKS = 8
OUTS = 2560
LIFT = 9

NT = (((1,), (1,)), ((), ()))
TN = (((0,), (0,)), ((), ()))
NN = (((1,), (0,)), ((), ()))


def iota(shape, axis):
    return lax.broadcasted_iota(jnp.int32, shape, axis)


def dot(a, b, dims=NN):
    return lax.dot_general(a, b, dims, preferred_element_type=F32)


def exact(a, b, dims=NN):
    return lax.dot_general(a, b, dims, precision=PRECISE, preferred_element_type=F32)


def split(value):
    high = value.astype(BF16)
    low = (value - high.astype(F32)).astype(BF16)
    return jnp.concatenate([high, low], axis=1)


def kernel(
    values,
    state_in,
    state_out,
    log_decay,
    level_class,
    level_table,
    skip_gain,
    norm_gain,
    weight,
    result,
    rows,
    entering,
    leaving,
    decay,
    classes,
    table,
    skip,
    gain,
    all_weight,
    expander,
    within,
    stretch,
    factors,
    totals,
    row_factors,
    mix_factors,
    pair_state,
    quad_state,
    half_state,
    output,
    ring_x,
    ring_z,
    buckets,
    normed_send,
    normed_all,
    own_sum,
    partial_send,
    partial_recv,
    local_sem,
    a_send,
    a_recv,
    w1_send,
    w1_recv,
    w2_send,
    w2_recv,
    wf_send,
    wf_recv,
    t_send,
    t_recv,
    x_send,
    x_recv,
    z_send,
    z_recv,
    n_send,
    n_recv,
    p_send,
    p_recv,
):
    ctx = lax.axis_index("ctx")
    head = lax.axis_index("head")
    x = lax.rem(ctx, 4)
    z = ctx // 4
    y = head // 2
    core = lax.rem(head, 2)
    partner = y * 2 + (1 - core)

    def copy(source, target, send, recv, device):
        return pltpu.make_async_remote_copy(
            src_ref=source,
            dst_ref=target,
            send_sem=send,
            recv_sem=recv,
            device_id=device,
            device_id_type=MESH,
        )

    loads = [
        pltpu.make_async_copy(source, target, local_sem.at[number])
        for number, (source, target) in enumerate(
            [
                (log_decay, decay),
                (level_class, classes),
                (level_table, table),
                (state_in, entering),
                (state_out, leaving),
                (skip_gain, skip),
                (norm_gain, gain),
            ]
        )
    ]
    for load in loads:
        load.start()
    own_lanes = pl.ds(pl.multiple_of(core * FEATS, LANES), FEATS)
    other_lanes = pl.ds(pl.multiple_of((1 - core) * FEATS, LANES), FEATS)
    own_rows = pltpu.make_async_copy(
        values.at[:, pl.ds(pl.multiple_of(head * FEATS, LANES), FEATS)],
        rows.at[head],
        local_sem.at[7],
    )
    own_rows.start()
    own_weight = pltpu.make_async_copy(
        weight, all_weight.at[z, x, :, :, own_lanes], local_sem.at[8]
    )
    own_weight.start()

    barrier = pltpu.get_barrier_semaphore()
    for step in range(1, 8):
        pl.semaphore_signal(
            barrier,
            inc=1,
            device_id=(ctx, lax.rem(head + step, 8)),
            device_id_type=MESH,
        )
    for step in range(1, 16):
        pl.semaphore_signal(
            barrier,
            inc=1,
            device_id=(lax.rem(ctx + step, 16), head),
            device_id_type=MESH,
        )
    pl.semaphore_wait(barrier, 22)

    def near_x(step):
        return z * 4 + lax.rem(x + step, 4)

    def near_z(step):
        return lax.rem(z + step, 4) * 4 + x

    offsets = [(0, 1), (1, 0), (1, 1), (3, 0), (3, 1), (2, 0), (2, 1)]
    order = [5, 6, 1, 2, 3, 4, 0]

    def head_at(step_y, step_core):
        return lax.rem(y + step_y, 4) * 2 + lax.rem(core + step_core, 2)

    value_copies = {}
    for number in order:
        step_y, step_core = offsets[number]
        target = head_at(step_y, step_core)
        value_copies[number] = copy(
            values.at[:, pl.ds(pl.multiple_of(target * FEATS, LANES), FEATS)],
            rows.at[head],
            a_send.at[number],
            a_recv.at[number],
            (ctx, target),
        )
        value_copies[number].start()

    first_copies = []
    for number, step in enumerate((2, 1, 3)):
        first_copies.append(
            copy(
                weight.at[0],
                all_weight.at[z, x, 0, :, own_lanes],
                w1_send.at[number],
                w1_recv.at[number],
                (near_x(step), head),
            )
        )
        first_copies.append(
            copy(
                weight.at[1],
                all_weight.at[z, x, 1, :, own_lanes],
                w1_send.at[3 + number],
                w1_recv.at[3 + number],
                (near_z(step), head),
            )
        )
    for item in first_copies:
        item.start()

    for load in loads:
        load.wait()
    spread = (
        (iota((HEADS_DEV, LANES), 1) % HEADS_DEV == iota((HEADS_DEV, LANES), 0))
        & (iota((HEADS_DEV, LANES), 1) < 100)
    ).astype(F32)
    lane_level = iota((CHUNK, LANES), 1) // HEADS_DEV
    causal = (iota((CHUNK, CHUNK), 0) >= iota((CHUNK, CHUNK), 1)) & (
        iota((CHUNK, CHUNK), 0) // 64 == iota((CHUNK, CHUNK), 1) // 64
    )
    causal_f32 = causal.astype(F32)
    first_half = iota((CHUNK, CHUNK), 1) < 64

    @pl.loop(0, CHUNKS)
    def _(j):
        tokens = pl.ds(pl.multiple_of(j * CHUNK, CHUNK), CHUNK)
        part = exact(causal_f32, exact(decay[tokens, :], spread))
        within[j] = part
        stretch[pl.ds(j * 2, 1), :] = part[63:64, :]
        stretch[pl.ds(j * 2 + 1, 1), :] = part[127:128, :]

    sums = stretch[...]
    total_row = jnp.sum(sums, axis=0, keepdims=True)
    totals[ctx] = jnp.broadcast_to(total_row, (8, LANES))
    total_copies = []
    for step in range(1, 16):
        total_copies.append(
            copy(
                totals.at[ctx],
                totals.at[ctx],
                t_send.at[step],
                t_recv.at[step],
                (lax.rem(ctx + step, 16), head),
            )
        )
        total_copies[-1].start()

    for level in range(10):
        source = iota((256, FEATS), 0) % LANES
        target = iota((256, FEATS), 1) // WIDTH + level * HEADS_DEV
        expander[level] = (source == target).astype(F32).astype(BF16)

    late = iota((16, 16), 0)
    early = iota((16, 16), 1)
    small_level = iota((16, LANES), 1) // HEADS_DEV
    prefix = jnp.zeros((16, LANES), F32)
    for size, low, high in ((2, 2, 3), (4, 3, 4), (8, 4, 5), (16, 5, 9)):
        before = ((late // size == early // size) & (early < late)).astype(F32)
        prefix = jnp.where(
            (small_level >= low) & (small_level < high), exact(before, sums), prefix
        )
    stretch[...] = prefix

    block = iota((32, 16), 0)
    piece = iota((32, 16), 1)
    pick = (block < 16) & (piece == block)
    pick = pick | (
        (block >= 16) & (block < 20) & (piece // 2 == (block - 16) * 2 + 1)
    )
    pick = pick | (
        (block >= 20) & (block < 22) & (piece // 4 == (block - 20) * 2 + 1)
    )
    pick = pick | ((block == 22) & (piece >= 8))
    row_factors[...] = dot(
        split(jnp.exp(exact(pick.astype(F32), sums))), expander[0]
    )

    table_rows = exact(
        table[:, 0, :], jnp.where(iota((HEADS_DEV, LANES), 1) // HEADS_DEV == 0, spread, 0.0)
    )
    for level in range(1, 9):
        table_rows = table_rows + exact(
            table[:, level, :],
            jnp.where(iota((HEADS_DEV, LANES), 1) // HEADS_DEV == level, spread, 0.0),
        )
    class_rows = iota((32, CHUNK), 0)
    lift_lane = (lane_level == LIFT).astype(F32)
    second_row = iota((CHUNK, LANES), 0) // 64

    @pl.loop(0, CHUNKS)
    def _(j):
        onehot = (class_rows == classes[pl.ds(j, 1), :]).astype(F32)
        weights = exact(onehot, table_rows, TN) + lift_lane
        part = within[j]
        start = jnp.where(
            second_row == 0, stretch[pl.ds(j * 2, 1), :], stretch[pl.ds(j * 2 + 1, 1), :]
        )
        exponent = jnp.where(lane_level == LIFT, -part, part + start)
        bit = jnp.where(
            lane_level == 1,
            second_row,
            jnp.where(
                lane_level == 2,
                lax.rem(j, 2),
                jnp.where(
                    lane_level == 3,
                    lax.rem(j // 2, 2),
                    jnp.where(lane_level == 4, j // 4, 1),
                ),
            ),
        )
        factors[j] = split(jnp.where(bit == 1, jnp.exp(exponent) * weights, 0.0))

    skip_row = dot(split(exact(skip[...], spread)), expander[0])

    own_weight.wait()
    for item in first_copies:
        item.wait_recv()
    second_copies = []
    forward_copies = []
    for number, step in enumerate((2, 1, 3)):
        second_copies.append(
            copy(
                all_weight.at[z, :, 0, :, own_lanes],
                all_weight.at[z, :, 0, :, own_lanes],
                w2_send.at[number],
                w2_recv.at[number],
                (near_z(step), head),
            )
        )
        second_copies.append(
            copy(
                all_weight.at[:, x, 1, :, own_lanes],
                all_weight.at[:, x, 1, :, own_lanes],
                w2_send.at[3 + number],
                w2_recv.at[3 + number],
                (near_x(step), head),
            )
        )
    for item in second_copies:
        item.start()

    def forward(slab, number):
        item = copy(
            slab(own_lanes),
            slab(own_lanes),
            wf_send.at[number],
            wf_recv.at[number],
            (ctx, partner),
        )
        item.start()
        forward_copies.append(item)

    forward(lambda lanes: all_weight.at[z, :, 0, :, lanes], 0)
    forward(lambda lanes: all_weight.at[:, x, 1, :, lanes], 1)

    def chunk_work(j):
        inputs = rows[j].astype(F32)
        factor = factors[j]
        tokens = pl.ds(pl.multiple_of(j * CHUNK, CHUNK), CHUNK)
        incoming = entering[tokens, :]
        reader = leaving[tokens, :]
        lifted = (dot(factor, expander[LIFT]) * inputs).astype(BF16)
        scores = jnp.where(causal, dot(reader, incoming, NT), 0.0)
        score_high = scores.astype(BF16)
        score_low = (scores - score_high.astype(F32)).astype(BF16)
        turned = incoming.astype(F32).T
        lower = jnp.where(first_half, turned, 0.0).astype(BF16)
        upper = jnp.where(first_half, 0.0, turned).astype(BF16)
        direct = dot(score_high, lifted) + dot(score_low, lifted)
        lower_state = row_factors[pl.ds(j * 2, 1), :] * dot(lower, lifted)
        pair_state[j] = row_factors[pl.ds(j * 2 + 1, 1), :] * (
            lower_state + dot(upper, lifted)
        )
        gained = dot(reader, lower_state.astype(BF16))
        output[j] = (
            dot(factor, expander[0]) * direct
            + dot(factor, expander[1]) * gained
            + skip_row * inputs
        )

    own_rows.wait()
    chunk_work(head)
    for number in range(7):
        step_y, step_core = offsets[number]
        origin = lax.rem(y + 4 - step_y, 4) * 2 + lax.rem(core + 2 - step_core, 2)
        copy(
            rows.at[origin],
            rows.at[origin],
            a_send.at[number],
            a_recv.at[number],
            (ctx, origin),
        ).wait_recv()

    @pl.loop(1, CHUNKS)
    def _(step):
        chunk_work(lax.rem(head + step, CHUNKS))

    for group in range(4):
        quad_state[group] = (
            row_factors[16 + group : 17 + group, :] * pair_state[2 * group]
            + pair_state[2 * group + 1]
        )
    for group in range(2):
        half_state[group] = (
            row_factors[20 + group : 21 + group, :] * quad_state[2 * group]
            + quad_state[2 * group + 1]
        )
    ring_x[x] = (row_factors[22:23, :] * half_state[0] + half_state[1]).astype(BF16)
    x_copies = []
    for number, step in enumerate((2, 1, 3)):
        x_copies.append(
            copy(
                ring_x.at[x],
                ring_x.at[x],
                x_send.at[number],
                x_recv.at[number],
                (near_x(step), head),
            )
        )
        x_copies[-1].start()

    @pl.loop(0, 4)
    def _(group):
        for level in (2, 3, 4):
            if level == 2:
                j = group * 2 + 1
                state = pair_state[group * 2]
            elif level == 3:
                j = 2 + lax.rem(group, 2) + 4 * (group // 2)
                state = quad_state[(group // 2) * 2]
            else:
                j = 4 + group
                state = half_state[0]
            tokens = pl.ds(pl.multiple_of(j * CHUNK, CHUNK), CHUNK)
            output[j] = output[j] + dot(factors[j], expander[level]) * dot(
                leaving[tokens, :], state.astype(BF16)
            )

    for step in range(1, 16):
        origin = lax.rem(ctx + 16 - step, 16)
        copy(
            totals.at[origin], totals.at[origin], t_send.at[step], t_recv.at[step], (origin, head)
        ).wait_recv()
    every_total = jnp.concatenate([totals[d][0:1, :] for d in range(16)], axis=0)
    row = iota((32, 16), 0)
    shard = iota((32, 16), 1)
    kind = row // 4
    slot = row % 4
    shard_x = shard % 4
    shard_z = shard // 4
    same_z = shard_z == z
    counted = ((kind == 1) & same_z & (shard_x > slot) & (shard_x < x)) | (
        (kind == 2) & same_z & (shard_x > slot)
    )
    counted = counted | ((kind >= 3) & (kind < 5) & same_z & (shard_x < x))
    counted = counted | ((kind == 4) & (shard_z > slot) & (shard_z < z))
    row = iota((32, LANES), 0)
    kind = row // 4
    slot = row % 4
    used = ((kind == 0) & (slot == x - 1) & (lax.rem(x, 2) == 1)) | (
        (kind == 1) & (x >= 2) & (slot < 2)
    )
    used = used | (kind == 2)
    used = used | ((kind == 3) & (slot == z - 1) & (lax.rem(z, 2) == 1))
    used = used | ((kind == 4) & (z >= 2) & (slot < 2))
    mix = jnp.where(used, jnp.exp(exact(counted.astype(F32), every_total)), 0.0)
    mix_factors[...] = dot(split(mix), expander[0])

    for number, step in enumerate((2, 1, 3)):
        origin = lax.rem(x + 4 - step, 4)
        copy(
            ring_x.at[origin],
            ring_x.at[origin],
            x_send.at[number],
            x_recv.at[number],
            (z * 4 + origin, head),
        ).wait_recv()
    first = jnp.zeros((STATE, FEATS), F32)
    second = jnp.zeros((STATE, FEATS), F32)
    merged = jnp.zeros((STATE, FEATS), F32)
    for source in range(4):
        state = ring_x[source].astype(F32)
        first = first + mix_factors[source : source + 1, :] * state
        second = second + mix_factors[4 + source : 5 + source, :] * state
        merged = merged + mix_factors[8 + source : 9 + source, :] * state
    ring_z[z] = merged.astype(BF16)
    z_copies = []
    for number, step in enumerate((2, 1, 3)):
        z_copies.append(
            copy(
                ring_z.at[z],
                ring_z.at[z],
                z_send.at[number],
                z_recv.at[number],
                (near_z(step), head),
            )
        )
        z_copies[-1].start()
    buckets[0] = first.astype(BF16)
    buckets[1] = second.astype(BF16)

    def read_levels(j, low):
        tokens = pl.ds(pl.multiple_of(j * CHUNK, CHUNK), CHUNK)
        reader = leaving[tokens, :]
        factor = factors[j]
        return dot(factor, expander[low]) * dot(reader, buckets[0]) + dot(
            factor, expander[low + 1]
        ) * dot(reader, buckets[1])

    @pl.loop(0, CHUNKS)
    def _(j):
        output[j] = output[j] + read_levels(j, 5)

    for number, step in enumerate((2, 1, 3)):
        from_z = lax.rem(z + 4 - step, 4)
        copy(
            all_weight.at[from_z, :, 0, :, own_lanes],
            all_weight.at[from_z, :, 0, :, own_lanes],
            w2_send.at[number],
            w2_recv.at[number],
            (from_z * 4 + x, head),
        ).wait_recv()
        forward(lambda lanes: all_weight.at[from_z, :, 0, :, lanes], 2 + number)
        from_x = lax.rem(x + 4 - step, 4)
        copy(
            all_weight.at[:, from_x, 1, :, own_lanes],
            all_weight.at[:, from_x, 1, :, own_lanes],
            w2_send.at[3 + number],
            w2_recv.at[3 + number],
            (z * 4 + from_x, head),
        ).wait_recv()
        forward(lambda lanes: all_weight.at[:, from_x, 1, :, lanes], 5 + number)

    for number, step in enumerate((2, 1, 3)):
        origin = lax.rem(z + 4 - step, 4)
        copy(
            ring_z.at[origin],
            ring_z.at[origin],
            z_send.at[number],
            z_recv.at[number],
            (origin * 4 + x, head),
        ).wait_recv()
    first = jnp.zeros((STATE, FEATS), F32)
    second = jnp.zeros((STATE, FEATS), F32)
    for source in range(4):
        state = ring_z[source].astype(F32)
        first = first + mix_factors[12 + source : 13 + source, :] * state
        second = second + mix_factors[16 + source : 17 + source, :] * state
    buckets[0] = first.astype(BF16)
    buckets[1] = second.astype(BF16)

    same_head = (
        iota((256, LANES), 0) % LANES // WIDTH == iota((256, LANES), 1) // WIDTH
    ).astype(F32).astype(BF16)

    def finish(j):
        total = output[j] + read_levels(j, 7)
        pieces = []
        for group in range(FEATS // LANES):
            part = total[:, group * LANES : (group + 1) * LANES]
            mean_square = dot(split(part * part), same_head) * (1.0 / WIDTH)
            scaled = part * lax.rsqrt(mean_square + EPSILON)
            pieces.append(scaled * gain[:, group * LANES : (group + 1) * LANES])
        return jnp.concatenate(pieces, axis=1).astype(BF16)

    @pl.loop(0, 4)
    def _(step):
        target = lax.rem(y + step, 4)
        normed_send[step] = finish(target * 2 + (1 - core))

    normed_copies = []
    for step in range(4):
        normed_copies.append(
            copy(
                normed_send.at[step],
                normed_all.at[step, :, own_lanes],
                n_send.at[step],
                n_recv.at[step],
                (ctx, partner),
            )
        )
        normed_copies[-1].start()

    @pl.loop(0, 4)
    def _(step):
        target = lax.rem(y + step, 4)
        normed_all[step, :, own_lanes] = finish(target * 2 + core)

    for item in normed_copies:
        item.wait_recv()

    slabs = [
        lambda lanes: all_weight.at[z, :, 0, :, lanes],
        lambda lanes: all_weight.at[:, x, 1, :, lanes],
    ]
    for number, step in enumerate((2, 1, 3)):
        from_z = lax.rem(z + 4 - step, 4)
        slabs.append(lambda lanes, at=from_z: all_weight.at[at, :, 0, :, lanes])
    for number, step in enumerate((2, 1, 3)):
        from_x = lax.rem(x + 4 - step, 4)
        slabs.append(lambda lanes, at=from_x: all_weight.at[:, at, 1, :, lanes])
    for number, slab in enumerate(slabs):
        copy(
            slab(other_lanes),
            slab(other_lanes),
            wf_send.at[number],
            wf_recv.at[number],
            (ctx, partner),
        ).wait_recv()

    tile = OUTS // 4
    partial_copies = []
    for quarter in range(4):
        block_weight = all_weight[quarter].reshape(tile, 2 * FEATS)
        product = dot(normed_all[...].reshape(4 * CHUNK, 2 * FEATS), block_weight, NT)
        own_sum[:, quarter * tile : (quarter + 1) * tile] = product[:CHUNK]
        for number, step in enumerate((2, 1, 3)):
            partial_send[number, quarter] = product[
                step * CHUNK : (step + 1) * CHUNK
            ].astype(BF16)
            item = copy(
                partial_send.at[number, quarter],
                partial_recv.at[number, quarter],
                p_send.at[number, quarter],
                p_recv.at[number, quarter],
                (ctx, lax.rem(y + step, 4) * 2 + core),
            )
            item.start()
            partial_copies.append(item)
    for quarter in range(4):
        for number in range(3):
            partial_copies[quarter * 3 + number].wait_recv()
        columns = slice(quarter * tile, (quarter + 1) * tile)
        result[:, columns] = (
            own_sum[:, columns]
            + partial_recv[0, quarter].astype(F32)
            + partial_recv[1, quarter].astype(F32)
            + partial_recv[2, quarter].astype(F32)
        ).astype(BF16)

    for number in order:
        value_copies[number].wait_send()
    for item in (
        first_copies
        + total_copies
        + second_copies
        + forward_copies
        + x_copies
        + z_copies
        + normed_copies
        + partial_copies
    ):
        item.wait_send()


def on_device(
    values,
    state_in,
    state_out,
    log_decay,
    level_class,
    level_table,
    skip_gain,
    norm_gain,
    out_weight,
):
    columns = out_weight.shape[1]
    weight = out_weight.T.reshape(2, columns // 2, FEATS)
    anywhere = pl.BlockSpec(memory_space=pl.ANY)
    dma = pltpu.SemaphoreType.DMA
    return pl.pallas_call(
        kernel,
        out_shape=jax.ShapeDtypeStruct((CHUNK, OUTS), BF16),
        in_specs=[anywhere] * 9,
        out_specs=pl.BlockSpec(memory_space=pltpu.VMEM),
        scratch_shapes=[
            pltpu.VMEM((CHUNKS, CHUNK, FEATS), BF16),
            pltpu.VMEM((CHUNKS * CHUNK, STATE), BF16),
            pltpu.VMEM((CHUNKS * CHUNK, STATE), BF16),
            pltpu.VMEM((CHUNKS * CHUNK, HEADS_DEV), F32),
            pltpu.VMEM((CHUNKS, CHUNK), jnp.int32),
            pltpu.VMEM((32, 9, HEADS_DEV), F32),
            pltpu.VMEM((1, HEADS_DEV), F32),
            pltpu.VMEM((1, FEATS), F32),
            pltpu.VMEM((4, 4, 2, 80, 2 * FEATS), BF16),
            pltpu.VMEM((10, 256, FEATS), BF16),
            pltpu.VMEM((CHUNKS, CHUNK, LANES), F32),
            pltpu.VMEM((16, LANES), F32),
            pltpu.VMEM((CHUNKS, CHUNK, 2 * LANES), BF16),
            pltpu.VMEM((16, 8, LANES), F32),
            pltpu.VMEM((32, FEATS), F32),
            pltpu.VMEM((32, FEATS), F32),
            pltpu.VMEM((CHUNKS, STATE, FEATS), F32),
            pltpu.VMEM((4, STATE, FEATS), F32),
            pltpu.VMEM((2, STATE, FEATS), F32),
            pltpu.VMEM((CHUNKS, CHUNK, FEATS), F32),
            pltpu.VMEM((4, STATE, FEATS), BF16),
            pltpu.VMEM((4, STATE, FEATS), BF16),
            pltpu.VMEM((2, STATE, FEATS), BF16),
            pltpu.VMEM((4, CHUNK, FEATS), BF16),
            pltpu.VMEM((4, CHUNK, 2 * FEATS), BF16),
            pltpu.VMEM((CHUNK, OUTS), F32),
            pltpu.VMEM((3, 4, CHUNK, OUTS // 4), BF16),
            pltpu.VMEM((3, 4, CHUNK, OUTS // 4), BF16),
            dma((9,)),
            dma((7,)),
            dma((7,)),
            dma((6,)),
            dma((6,)),
            dma((6,)),
            dma((6,)),
            dma((8,)),
            dma((8,)),
            dma((16,)),
            dma((16,)),
            dma((3,)),
            dma((3,)),
            dma((3,)),
            dma((3,)),
            dma((4,)),
            dma((4,)),
            dma((3, 4)),
            dma((3, 4)),
        ],
        compiler_params=pltpu.CompilerParams(
            collective_id=0,
            has_side_effects=True,
            vmem_limit_bytes=60 * 1024 * 1024,
        ),
        name="layer",
    )(
        values,
        state_in,
        state_out,
        log_decay,
        level_class.reshape(CHUNKS, CHUNK),
        level_table,
        skip_gain.reshape(1, -1),
        norm_gain.reshape(1, -1),
        weight,
    )


def solution(mesh):
    return jax.shard_map(
        on_device,
        mesh=mesh,
        in_specs=(
            P(("ctx", "head"), None),
            P("ctx", None),
            P("ctx", None),
            P("ctx", "head"),
            P("ctx"),
            P(None, None, "head"),
            P("head"),
            P("head"),
            P("head", "ctx"),
        ),
        out_specs=P(("ctx", "head"), None),
        check_vma=False,
    )
```

```python
import jax
import jax.numpy as jnp
from jax import lax
from jax.experimental import pallas as pl
from jax.experimental.pallas import tpu as pltpu
from jax.sharding import PartitionSpec as P

MESH = pl.DeviceIdType.MESH
PRECISE = lax.Precision.HIGHEST
EPSILON = 1e-05
F32 = jnp.float32
BF16 = jnp.bfloat16
LANES = 128
HEADS_DEV = 10
WIDTH = 64
FEATS = HEADS_DEV * WIDTH
STATE = 128
CHUNK = 128
CHUNKS = 8
OUTS = 2560
LIFT = 9
GROUPS = ((0, 384), (384, 640))
TILE = OUTS // 4

NT = (((1,), (1,)), ((), ()))
TN = (((0,), (0,)), ((), ()))
NN = (((1,), (0,)), ((), ()))


def iota(shape, axis):
    return lax.broadcasted_iota(jnp.int32, shape, axis)


def dot(a, b, dims=NN):
    return lax.dot_general(a, b, dims, preferred_element_type=F32)


def exact(a, b, dims=NN):
    return lax.dot_general(a, b, dims, precision=PRECISE, preferred_element_type=F32)


def split(value, axis=1):
    high = value.astype(BF16)
    low = (value - high.astype(F32)).astype(BF16)
    return jnp.concatenate([high, low], axis=axis)


def kernel(
    values,
    state_in,
    state_out,
    log_decay,
    level_class,
    level_table,
    skip_gain,
    norm_gain,
    weight,
    result,
    rows,
    entering,
    leaving,
    decay,
    classes,
    table,
    skip,
    gain,
    all_weight,
    expander,
    within,
    stretch,
    factors,
    mixers,
    readers,
    totals,
    row_factors,
    mix_factors,
    pair_state,
    quad_state,
    half_state,
    output,
    ring_x,
    ring_z,
    buckets,
    normed_send,
    normed_all,
    own_sum,
    held,
    partial_send,
    relay_recv,
    partial_recv,
    local_sem,
    a_send,
    a_recv,
    w1_send,
    w1_recv,
    w2_send,
    w2_recv,
    wf_send,
    wf_recv,
    t_send,
    t_recv,
    x_send,
    x_recv,
    z_send,
    z_recv,
    n_send,
    n_recv,
    r_send,
    r_recv,
    p_send,
    p_recv,
):
    ctx = lax.axis_index("ctx")
    head = lax.axis_index("head")
    x = lax.rem(ctx, 4)
    z = ctx // 4
    y = head // 2
    core = lax.rem(head, 2)
    partner = y * 2 + (1 - core)

    def copy(source, target, send, recv, device):
        return pltpu.make_async_remote_copy(
            src_ref=source,
            dst_ref=target,
            send_sem=send,
            recv_sem=recv,
            device_id=device,
            device_id_type=MESH,
        )

    loads = [
        pltpu.make_async_copy(source, target, local_sem.at[number])
        for number, (source, target) in enumerate(
            [
                (log_decay, decay),
                (level_class, classes),
                (level_table, table),
                (state_in, entering),
                (state_out, leaving),
                (skip_gain, skip),
                (norm_gain, gain),
            ]
        )
    ]
    for load in loads:
        load.start()
    own_lanes = pl.ds(pl.multiple_of(core * FEATS, LANES), FEATS)
    other_lanes = pl.ds(pl.multiple_of((1 - core) * FEATS, LANES), FEATS)
    for number, (low, high) in enumerate(GROUPS):
        pltpu.make_async_copy(
            values.at[:, pl.ds(pl.multiple_of(head * FEATS + low, LANES), high - low)],
            rows.at[head, :, low:high],
            a_recv.at[number, 0],
        ).start()
    own_weight = pltpu.make_async_copy(
        weight, all_weight.at[z, x, :, :, own_lanes], local_sem.at[7]
    )
    own_weight.start()

    barrier = pltpu.get_barrier_semaphore()
    for step in range(1, 8):
        pl.semaphore_signal(
            barrier,
            inc=1,
            device_id=(ctx, lax.rem(head + step, 8)),
            device_id_type=MESH,
        )
    for step in range(1, 16):
        pl.semaphore_signal(
            barrier,
            inc=1,
            device_id=(lax.rem(ctx + step, 16), head),
            device_id_type=MESH,
        )
    pl.semaphore_wait(barrier, 22)

    def near_x(step):
        return z * 4 + lax.rem(x + step, 4)

    def near_z(step):
        return lax.rem(z + step, 4) * 4 + x

    def step_of(number):
        pair = number // 2
        return pair + (pair // 2) * (1 - 2 * lax.rem(pair, 2)), lax.rem(number, 2)

    value_copies = []
    for group, (low, high) in enumerate(GROUPS):
        for number in (6, 7, 2, 3, 4, 5, 1):
            step_y, step_core = step_of(number)
            target = lax.rem(y + step_y, 4) * 2 + lax.rem(core + step_core, 2)
            value_copies.append(
                copy(
                    values.at[
                        :, pl.ds(pl.multiple_of(target * FEATS + low, LANES), high - low)
                    ],
                    rows.at[head, :, low:high],
                    a_send.at[group, number],
                    a_recv.at[group, number],
                    (ctx, target),
                )
            )
            value_copies[-1].start()

    first_copies = []
    for number, step in enumerate((2, 1, 3)):
        first_copies.append(
            copy(
                weight.at[0],
                all_weight.at[z, x, 0, :, own_lanes],
                w1_send.at[number],
                w1_recv.at[number],
                (near_x(step), head),
            )
        )
        first_copies.append(
            copy(
                weight.at[1],
                all_weight.at[z, x, 1, :, own_lanes],
                w1_send.at[3 + number],
                w1_recv.at[3 + number],
                (near_z(step), head),
            )
        )
    for item in first_copies:
        item.start()

    for load in loads:
        load.wait()
    spread = (
        (iota((HEADS_DEV, LANES), 1) % HEADS_DEV == iota((HEADS_DEV, LANES), 0))
        & (iota((HEADS_DEV, LANES), 1) < 100)
    ).astype(F32)
    lane_level = iota((CHUNK, LANES), 1) // HEADS_DEV
    causal = (iota((CHUNK, CHUNK), 0) >= iota((CHUNK, CHUNK), 1)) & (
        iota((CHUNK, CHUNK), 0) // 64 == iota((CHUNK, CHUNK), 1) // 64
    )
    causal_f32 = causal.astype(F32)
    first_half = iota((CHUNK, CHUNK), 1) < 64

    @pl.loop(0, CHUNKS)
    def _(j):
        tokens = pl.ds(pl.multiple_of(j * CHUNK, CHUNK), CHUNK)
        part = exact(causal_f32, exact(decay[:, tokens], spread, TN))
        within[j] = part
        stretch[pl.ds(j * 2, 1), :] = part[63:64, :]
        stretch[pl.ds(j * 2 + 1, 1), :] = part[127:128, :]

    sums = stretch[...]
    total_row = jnp.sum(sums, axis=0, keepdims=True)
    totals[ctx] = jnp.broadcast_to(total_row, (8, LANES))
    total_copies = []
    for step in range(1, 16):
        total_copies.append(
            copy(
                totals.at[ctx],
                totals.at[ctx],
                t_send.at[step],
                t_recv.at[step],
                (lax.rem(ctx + step, 16), head),
            )
        )
        total_copies[-1].start()

    for level in range(10):
        source = iota((256, FEATS), 0) % LANES
        target = iota((256, FEATS), 1) // WIDTH + level * HEADS_DEV
        expander[level] = (source == target).astype(F32).astype(BF16)

    late = iota((16, 16), 0)
    early = iota((16, 16), 1)
    small_level = iota((16, LANES), 1) // HEADS_DEV
    prefix = jnp.zeros((16, LANES), F32)
    for size, low, high in ((2, 2, 3), (4, 3, 4), (8, 4, 5), (16, 5, 9)):
        before = ((late // size == early // size) & (early < late)).astype(F32)
        prefix = jnp.where(
            (small_level >= low) & (small_level < high), exact(before, sums), prefix
        )
    stretch[...] = prefix

    block = iota((32, 16), 0)
    piece = iota((32, 16), 1)
    pick = (block < 16) & (piece == block)
    pick = pick | (
        (block >= 16) & (block < 20) & (piece // 2 == (block - 16) * 2 + 1)
    )
    pick = pick | (
        (block >= 20) & (block < 22) & (piece // 4 == (block - 20) * 2 + 1)
    )
    pick = pick | ((block == 22) & (piece >= 8))
    row_factors[...] = dot(
        split(jnp.exp(exact(pick.astype(F32), sums))), expander[0]
    )

    table_rows = jnp.zeros((32, LANES), F32)
    for level in range(9):
        table_rows = table_rows + exact(
            table[level],
            jnp.where(iota((HEADS_DEV, LANES), 1) // HEADS_DEV == level, spread, 0.0),
            TN,
        )
    class_rows = iota((32, CHUNK), 0)
    lift_lane = (lane_level == LIFT).astype(F32)
    second_row = iota((CHUNK, LANES), 0) // 64

    @pl.loop(0, CHUNKS)
    def _(j):
        onehot = (class_rows == classes[pl.ds(j, 1), :]).astype(F32)
        weights = exact(onehot, table_rows, TN) + lift_lane
        part = within[j]
        start = jnp.where(
            second_row == 0, stretch[pl.ds(j * 2, 1), :], stretch[pl.ds(j * 2 + 1, 1), :]
        )
        exponent = jnp.where(lane_level == LIFT, -part, part + start)
        bit = jnp.where(
            lane_level == 1,
            second_row,
            jnp.where(
                lane_level == 2,
                lax.rem(j, 2),
                jnp.where(
                    lane_level == 3,
                    lax.rem(j // 2, 2),
                    jnp.where(lane_level == 4, j // 4, 1),
                ),
            ),
        )
        factors[j] = split(jnp.where(bit == 1, jnp.exp(exponent) * weights, 0.0))
        tokens = pl.ds(pl.multiple_of(j * CHUNK, CHUNK), CHUNK)
        incoming = entering[tokens, :]
        reader = leaving[tokens, :]
        readers[j] = jnp.concatenate([reader, reader], axis=1)
        scores = jnp.where(causal, dot(reader, incoming, NT), 0.0)
        score_high = scores.astype(BF16)
        score_low = (scores - score_high.astype(F32)).astype(BF16)
        turned = incoming.astype(F32).T
        lower = jnp.where(first_half, turned, 0.0).astype(BF16)
        upper = jnp.where(first_half, 0.0, turned).astype(BF16)
        half = jnp.concatenate([score_high, score_low, lower, upper], axis=0)
        mixers[j] = jnp.concatenate([half, half], axis=1)

    skip_row = dot(split(exact(skip[...], spread)), expander[0])

    own_weight.wait()
    for item in first_copies:
        item.wait_recv()
    second_copies = []
    forward_copies = []
    for number, step in enumerate((2, 1, 3)):
        second_copies.append(
            copy(
                all_weight.at[z, :, 0, :, own_lanes],
                all_weight.at[z, :, 0, :, own_lanes],
                w2_send.at[number],
                w2_recv.at[number],
                (near_z(step), head),
            )
        )
        second_copies.append(
            copy(
                all_weight.at[:, x, 1, :, own_lanes],
                all_weight.at[:, x, 1, :, own_lanes],
                w2_send.at[3 + number],
                w2_recv.at[3 + number],
                (near_x(step), head),
            )
        )
    for item in second_copies:
        item.start()

    def forward(slab, number):
        item = copy(
            slab(own_lanes),
            slab(own_lanes),
            wf_send.at[number],
            wf_recv.at[number],
            (ctx, partner),
        )
        item.start()
        forward_copies.append(item)

    forward(lambda lanes: all_weight.at[z, :, 0, :, lanes], 0)
    forward(lambda lanes: all_weight.at[:, x, 1, :, lanes], 1)

    def chunk_work(j, low, high):
        inputs = rows[j, :, low:high].astype(F32)
        factor = factors[j]
        lifted = split(dot(factor, expander[LIFT, :, low:high]) * inputs, 0)
        product = dot(mixers[j], lifted)
        lower_state = row_factors[pl.ds(j * 2, 1), low:high] * product[256:384]
        pair_state[j, :, low:high] = row_factors[pl.ds(j * 2 + 1, 1), low:high] * (
            lower_state + product[384:512]
        )
        gained = dot(readers[j], split(lower_state, 0))
        output[j, :, low:high] = (
            dot(factor, expander[0, :, low:high]) * (product[:128] + product[128:256])
            + dot(factor, expander[1, :, low:high]) * gained
            + skip_row[:, low:high] * inputs
        )

    x_copies = []
    for group, (low, high) in enumerate(GROUPS):

        @pl.loop(0, CHUNKS)
        def _(number):
            step_y, step_core = step_of(number)
            origin = lax.rem(y + 4 - step_y, 4) * 2 + lax.rem(core + 2 - step_core, 2)
            pltpu.make_async_copy(
                rows.at[origin, :, low:high],
                rows.at[origin, :, low:high],
                a_recv.at[group, number],
            ).wait()
            chunk_work(origin, low, high)

        for quad in range(4):
            quad_state[quad, :, low:high] = (
                row_factors[16 + quad : 17 + quad, low:high]
                * pair_state[2 * quad, :, low:high]
                + pair_state[2 * quad + 1, :, low:high]
            )
        for half in range(2):
            half_state[half, :, low:high] = (
                row_factors[20 + half : 21 + half, low:high]
                * quad_state[2 * half, :, low:high]
                + quad_state[2 * half + 1, :, low:high]
            )
        ring_x[x, :, low:high] = (
            row_factors[22:23, low:high] * half_state[0, :, low:high]
            + half_state[1, :, low:high]
        ).astype(BF16)
        for number, step in enumerate((2, 1, 3)):
            x_copies.append(
                copy(
                    ring_x.at[x, :, low:high],
                    ring_x.at[x, :, low:high],
                    x_send.at[group, number],
                    x_recv.at[group, number],
                    (near_x(step), head),
                )
            )
            x_copies[-1].start()
        if group == 0:
            for step in range(1, 16):
                origin = lax.rem(ctx + 16 - step, 16)
                copy(
                    totals.at[origin],
                    totals.at[origin],
                    t_send.at[step],
                    t_recv.at[step],
                    (origin, head),
                ).wait_recv()
            every_total = jnp.concatenate([totals[d][0:1, :] for d in range(16)], axis=0)
            row = iota((32, 16), 0)
            shard = iota((32, 16), 1)
            kind = row // 4
            slot = row % 4
            shard_x = shard % 4
            shard_z = shard // 4
            same_z = shard_z == z
            counted = (kind == 1) & same_z & (shard_x > slot) & (shard_x < x)
            counted = counted | ((kind == 2) & same_z & (shard_x > slot))
            counted = counted | ((kind >= 3) & (kind < 5) & same_z & (shard_x < x))
            counted = counted | ((kind == 4) & (shard_z > slot) & (shard_z < z))
            row = iota((32, LANES), 0)
            kind = row // 4
            slot = row % 4
            used = (kind == 0) & (slot == x - 1) & (lax.rem(x, 2) == 1)
            used = used | ((kind == 1) & (x >= 2) & (slot < 2))
            used = used | (kind == 2)
            used = used | ((kind == 3) & (slot == z - 1) & (lax.rem(z, 2) == 1))
            used = used | ((kind == 4) & (z >= 2) & (slot < 2))
            mix = jnp.where(used, jnp.exp(exact(counted.astype(F32), every_total)), 0.0)
            mix_factors[...] = dot(split(mix), expander[0])

    def mixed(ring, start, low, high):
        total = jnp.zeros((STATE, high - low), F32)
        for source in range(4):
            total = total + mix_factors[
                start + source : start + source + 1, low:high
            ] * ring[source, :, low:high].astype(F32)
        return total

    def hear(ring, recv, group, low, high, position, device):
        for number, step in enumerate((2, 1, 3)):
            origin = lax.rem(position + 4 - step, 4)
            copy(
                ring.at[origin, :, low:high],
                ring.at[origin, :, low:high],
                x_send.at[group, number],
                recv.at[group, number],
                (device(origin), head),
            ).wait_recv()

    def read_local(group):
        for level in (2, 3, 4):
            if level == 2:
                j = group * 2 + 1
                state = pair_state[group * 2]
            elif level == 3:
                j = 2 + lax.rem(group, 2) + 4 * (group // 2)
                state = quad_state[(group // 2) * 2]
            else:
                j = 4 + group
                state = half_state[0]
            output[j] = output[j] + dot(factors[j], expander[level]) * dot(
                readers[j], split(state, 0)
            )

    z_copies = []
    for group, (low, high) in enumerate(GROUPS):
        hear(ring_x, x_recv, group, low, high, x, lambda origin: z * 4 + origin)
        ring_z[z, :, low:high] = mixed(ring_x, 8, low, high).astype(BF16)
        for number, step in enumerate((2, 1, 3)):
            z_copies.append(
                copy(
                    ring_z.at[z, :, low:high],
                    ring_z.at[z, :, low:high],
                    z_send.at[group, number],
                    z_recv.at[group, number],
                    (near_z(step), head),
                )
            )
            z_copies[-1].start()
        buckets[0, :, low:high] = split(mixed(ring_x, 0, low, high), 0)
        buckets[1, :, low:high] = split(mixed(ring_x, 4, low, high), 0)
        if group == 0:
            pl.loop(0, 4)(read_local)

    def read_levels(j, low):
        factor = factors[j]
        reader = readers[j]
        return dot(factor, expander[low]) * dot(reader, buckets[0]) + dot(
            factor, expander[low + 1]
        ) * dot(reader, buckets[1])

    @pl.loop(0, CHUNKS)
    def _(j):
        output[j] = output[j] + read_levels(j, 5)

    for number, step in enumerate((2, 1, 3)):
        from_z = lax.rem(z + 4 - step, 4)
        copy(
            all_weight.at[from_z, :, 0, :, own_lanes],
            all_weight.at[from_z, :, 0, :, own_lanes],
            w2_send.at[number],
            w2_recv.at[number],
            (from_z * 4 + x, head),
        ).wait_recv()
        forward(lambda lanes: all_weight.at[from_z, :, 0, :, lanes], 2 + number)
        from_x = lax.rem(x + 4 - step, 4)
        copy(
            all_weight.at[:, from_x, 1, :, own_lanes],
            all_weight.at[:, from_x, 1, :, own_lanes],
            w2_send.at[3 + number],
            w2_recv.at[3 + number],
            (z * 4 + from_x, head),
        ).wait_recv()
        forward(lambda lanes: all_weight.at[:, from_x, 1, :, lanes], 5 + number)

    for group, (low, high) in enumerate(GROUPS):
        hear(ring_z, z_recv, group, low, high, z, lambda origin: origin * 4 + x)
        buckets[0, :, low:high] = split(mixed(ring_z, 12, low, high), 0)
        buckets[1, :, low:high] = split(mixed(ring_z, 16, low, high), 0)

    same_head = (
        iota((256, LANES), 0) % LANES // WIDTH == iota((256, LANES), 1) // WIDTH
    ).astype(F32).astype(BF16)

    def finish(j):
        total = output[j] + read_levels(j, 7)
        pieces = []
        for group in range(FEATS // LANES):
            part = total[:, group * LANES : (group + 1) * LANES]
            mean_square = dot(split(part * part), same_head) * (1.0 / WIDTH)
            scaled = part * lax.rsqrt(mean_square + EPSILON)
            pieces.append(scaled * gain[:, group * LANES : (group + 1) * LANES])
        return jnp.concatenate(pieces, axis=1).astype(BF16)

    def place_chip(place):
        return lax.rem(y + (2, 1, 3, 0)[place], 4)

    normed_copies = []

    def hand_over(place):
        normed_send[place] = finish(place_chip(place) * 2 + (1 - core))
        normed_copies.append(
            copy(
                normed_send.at[place],
                normed_all.at[place, :, own_lanes],
                n_send.at[place],
                n_recv.at[place],
                (ctx, partner),
            )
        )
        normed_copies[-1].start()

    def keep(place):
        normed_all[place, :, own_lanes] = finish(place_chip(place) * 2 + core)

    hand_over(0)
    keep(0)
    hand_over(1)
    slabs = [
        lambda lanes: all_weight.at[z, :, 0, :, lanes],
        lambda lanes: all_weight.at[:, x, 1, :, lanes],
    ]
    for number, step in enumerate((2, 1, 3)):
        from_z = lax.rem(z + 4 - step, 4)
        slabs.append(lambda lanes, at=from_z: all_weight.at[at, :, 0, :, lanes])
    for number, step in enumerate((2, 1, 3)):
        from_x = lax.rem(x + 4 - step, 4)
        slabs.append(lambda lanes, at=from_x: all_weight.at[:, at, 1, :, lanes])
    for number, slab in enumerate(slabs):
        copy(
            slab(other_lanes),
            slab(other_lanes),
            wf_send.at[number],
            wf_recv.at[number],
            (ctx, partner),
        ).wait_recv()

    up = (ctx, lax.rem(y + 1, 4) * 2 + core)
    down = (ctx, lax.rem(y + 3, 4) * 2 + core)
    partial_copies = []

    def product(first_place, last_place, quarter):
        count = last_place - first_place
        return dot(
            normed_all[first_place:last_place].reshape(count * CHUNK, 2 * FEATS),
            all_weight[quarter].reshape(TILE, 2 * FEATS),
            NT,
        )

    def send(value, place, quarter, target, send_sems, recv_sems, device):
        partial_send[place, quarter] = value.astype(BF16)
        item = copy(
            partial_send.at[place, quarter], target, send_sems, recv_sems, device
        )
        item.start()
        partial_copies.append(item)

    normed_copies[0].wait_recv()
    for quarter in (0, 2, 1, 3):
        send(
            product(0, 1, quarter),
            0,
            quarter,
            relay_recv.at[quarter],
            r_send.at[quarter],
            r_recv.at[quarter],
            up if quarter < 2 else down,
        )
    keep(1)
    hand_over(2)
    keep(2)
    normed_copies[1].wait_recv()
    normed_copies[2].wait_recv()

    def send_near(value, place, quarter):
        send(
            value,
            place,
            quarter,
            partial_recv.at[place - 1, quarter],
            p_send.at[place - 1, quarter],
            p_recv.at[place - 1, quarter],
            up if place == 1 else down,
        )

    for quarter in (2, 0, 3, 1):
        both = product(1, 3, quarter)
        if quarter < 2:
            held[quarter] = both[:CHUNK]
            send_near(both[CHUNK:], 2, quarter)
        else:
            send_near(both[:CHUNK], 1, quarter)
            held[quarter] = both[CHUNK:]
    hand_over(3)
    keep(3)
    for quarter in (0, 2, 1, 3):
        partial_copies[(0, 2, 1, 3).index(quarter)].wait_recv()
        send_near(
            held[quarter] + relay_recv[quarter].astype(F32),
            1 if quarter < 2 else 2,
            quarter,
        )
    normed_copies[3].wait_recv()
    for quarter in range(4):
        own_sum[:, quarter * TILE : (quarter + 1) * TILE] = product(3, 4, quarter)
    for quarter in range(4):
        for place in range(2):
            copy(
                partial_recv.at[place, quarter],
                partial_recv.at[place, quarter],
                p_send.at[place, quarter],
                p_recv.at[place, quarter],
                up,
            ).wait_recv()
        columns = slice(quarter * TILE, (quarter + 1) * TILE)
        result[:, columns] = (
            own_sum[:, columns]
            + partial_recv[0, quarter].astype(F32)
            + partial_recv[1, quarter].astype(F32)
        ).astype(BF16)

    for item in (
        value_copies
        + first_copies
        + total_copies
        + second_copies
        + forward_copies
        + x_copies
        + z_copies
        + normed_copies
        + partial_copies
    ):
        item.wait_send()


def on_device(
    values,
    state_in,
    state_out,
    log_decay,
    level_class,
    level_table,
    skip_gain,
    norm_gain,
    out_weight,
):
    columns = out_weight.shape[1]
    weight = out_weight.T.reshape(2, columns // 2, FEATS)
    anywhere = pl.BlockSpec(memory_space=pl.ANY)
    dma = pltpu.SemaphoreType.DMA
    groups = len(GROUPS)
    return pl.pallas_call(
        kernel,
        out_shape=jax.ShapeDtypeStruct((CHUNK, OUTS), BF16),
        in_specs=[anywhere] * 9,
        out_specs=pl.BlockSpec(memory_space=pltpu.VMEM),
        scratch_shapes=[
            pltpu.VMEM((CHUNKS, CHUNK, FEATS), BF16),
            pltpu.VMEM((CHUNKS * CHUNK, STATE), BF16),
            pltpu.VMEM((CHUNKS * CHUNK, STATE), BF16),
            pltpu.VMEM((HEADS_DEV, CHUNKS * CHUNK), F32),
            pltpu.VMEM((CHUNKS, CHUNK), jnp.int32),
            pltpu.VMEM((9, HEADS_DEV, 32), F32),
            pltpu.VMEM((1, HEADS_DEV), F32),
            pltpu.VMEM((1, FEATS), F32),
            pltpu.VMEM((4, 4, 2, 80, 2 * FEATS), BF16),
            pltpu.VMEM((10, 256, FEATS), BF16),
            pltpu.VMEM((CHUNKS, CHUNK, LANES), F32),
            pltpu.VMEM((16, LANES), F32),
            pltpu.VMEM((CHUNKS, CHUNK, 2 * LANES), BF16),
            pltpu.VMEM((CHUNKS, 4 * CHUNK, 2 * STATE), BF16),
            pltpu.VMEM((CHUNKS, CHUNK, 2 * STATE), BF16),
            pltpu.VMEM((16, 8, LANES), F32),
            pltpu.VMEM((32, FEATS), F32),
            pltpu.VMEM((32, FEATS), F32),
            pltpu.VMEM((CHUNKS, STATE, FEATS), F32),
            pltpu.VMEM((4, STATE, FEATS), F32),
            pltpu.VMEM((2, STATE, FEATS), F32),
            pltpu.VMEM((CHUNKS, CHUNK, FEATS), F32),
            pltpu.VMEM((4, STATE, FEATS), BF16),
            pltpu.VMEM((4, STATE, FEATS), BF16),
            pltpu.VMEM((2, 2 * STATE, FEATS), BF16),
            pltpu.VMEM((4, CHUNK, FEATS), BF16),
            pltpu.VMEM((4, CHUNK, 2 * FEATS), BF16),
            pltpu.VMEM((CHUNK, OUTS), F32),
            pltpu.VMEM((4, CHUNK, TILE), F32),
            pltpu.VMEM((3, 4, CHUNK, TILE), BF16),
            pltpu.VMEM((4, CHUNK, TILE), BF16),
            pltpu.VMEM((2, 4, CHUNK, TILE), BF16),
            dma((8,)),
            dma((groups, 8)),
            dma((groups, 8)),
            dma((6,)),
            dma((6,)),
            dma((6,)),
            dma((6,)),
            dma((8,)),
            dma((8,)),
            dma((16,)),
            dma((16,)),
            dma((groups, 3)),
            dma((groups, 3)),
            dma((groups, 3)),
            dma((groups, 3)),
            dma((4,)),
            dma((4,)),
            dma((4,)),
            dma((4,)),
            dma((2, 4)),
            dma((2, 4)),
        ],
        compiler_params=pltpu.CompilerParams(
            collective_id=0,
            has_side_effects=True,
            vmem_limit_bytes=60 * 1024 * 1024,
        ),
        name="layer",
    )(
        values,
        state_in,
        state_out,
        log_decay.T,
        level_class.reshape(CHUNKS, CHUNK),
        level_table.transpose(1, 2, 0),
        skip_gain.reshape(1, -1),
        norm_gain.reshape(1, -1),
        weight,
    )


def solution(mesh):
    return jax.shard_map(
        on_device,
        mesh=mesh,
        in_specs=(
            P(("ctx", "head"), None),
            P("ctx", None),
            P("ctx", None),
            P("ctx", "head"),
            P("ctx"),
            P(None, None, "head"),
            P("head"),
            P("head"),
            P("head", "ctx"),
        ),
        out_specs=P(("ctx", "head"), None),
        check_vma=False,
    )
```

```python
import jax
import jax.numpy as jnp
from jax import lax
from jax.experimental import pallas as pl
from jax.experimental.pallas import tpu as pltpu
from jax.sharding import PartitionSpec as P

MESH = pl.DeviceIdType.MESH
PRECISE = lax.Precision.HIGHEST
EPSILON = 1e-05
F32 = jnp.float32
BF16 = jnp.bfloat16
LANES = 128
HEADS_DEV = 10
WIDTH = 64
FEATS = HEADS_DEV * WIDTH
STATE = 128
CHUNK = 128
CHUNKS = 8
OUTS = 2560
LIFT = 9
GROUPS = ((0, 384), (384, 640))
TILE = OUTS // 4

NT = (((1,), (1,)), ((), ()))
TN = (((0,), (0,)), ((), ()))
NN = (((1,), (0,)), ((), ()))


def iota(shape, axis):
    return lax.broadcasted_iota(jnp.int32, shape, axis)


def dot(a, b, dims=NN):
    return lax.dot_general(a, b, dims, preferred_element_type=F32)


def exact(a, b, dims=NN):
    return lax.dot_general(a, b, dims, precision=PRECISE, preferred_element_type=F32)


def split(value, axis=1):
    high = value.astype(BF16)
    low = (value - high.astype(F32)).astype(BF16)
    return jnp.concatenate([high, low], axis=axis)


def split3(value):
    high = value.astype(BF16)
    rest = value - high.astype(F32)
    middle = rest.astype(BF16)
    return high, middle, (rest - middle.astype(F32)).astype(BF16)


def kernel(
    values,
    state_in,
    state_out,
    log_decay,
    level_class,
    level_table,
    skip_gain,
    norm_gain,
    weight,
    result,
    rows,
    entering,
    leaving,
    decay,
    classes,
    table,
    skip,
    gain,
    all_weight,
    expander,
    within,
    stretch,
    factors,
    mixers,
    readers,
    totals,
    row_factors,
    mix_factors,
    pair_state,
    quad_state,
    half_state,
    output,
    ring_x,
    ring_z,
    buckets,
    normed_send,
    normed_all,
    own_sum,
    held,
    partial_send,
    relay_recv,
    partial_recv,
    local_sem,
    a_send,
    a_recv,
    w1_send,
    w1_recv,
    w2_send,
    w2_recv,
    wf_send,
    wf_recv,
    t_send,
    t_recv,
    x_send,
    x_recv,
    z_send,
    z_recv,
    n_send,
    n_recv,
    r_send,
    r_recv,
    p_send,
    p_recv,
):
    ctx = lax.axis_index("ctx")
    head = lax.axis_index("head")
    x = lax.rem(ctx, 4)
    z = ctx // 4
    y = head // 2
    core = lax.rem(head, 2)
    partner = y * 2 + (1 - core)

    def copy(source, target, send, recv, device):
        return pltpu.make_async_remote_copy(
            src_ref=source,
            dst_ref=target,
            send_sem=send,
            recv_sem=recv,
            device_id=device,
            device_id_type=MESH,
        )

    loads = [
        pltpu.make_async_copy(source, target, local_sem.at[number])
        for number, (source, target) in enumerate(
            [
                (log_decay, decay),
                (level_class, classes),
                (level_table, table),
                (state_in, entering),
                (state_out, leaving),
                (skip_gain, skip),
                (norm_gain, gain),
            ]
        )
    ]
    for load in loads:
        load.start()
    own_lanes = pl.ds(pl.multiple_of(core * FEATS, LANES), FEATS)
    other_lanes = pl.ds(pl.multiple_of((1 - core) * FEATS, LANES), FEATS)
    my_rows = pl.ds(pl.multiple_of(core * CHUNK, CHUNK), CHUNK)
    for group, (low, high) in enumerate(GROUPS):
        pltpu.make_async_copy(
            values.at[:, pl.ds(pl.multiple_of(head * FEATS + low, LANES), high - low)],
            rows.at[y, my_rows, low:high],
            a_recv.at[group, 0],
        ).start()
    own_weight = pltpu.make_async_copy(
        weight, all_weight.at[z, x, :, :, own_lanes], local_sem.at[7]
    )
    own_weight.start()

    barrier = pltpu.get_barrier_semaphore()
    for step in range(1, 8):
        pl.semaphore_signal(
            barrier,
            inc=1,
            device_id=(ctx, lax.rem(head + step, 8)),
            device_id_type=MESH,
        )
    for step in range(1, 16):
        pl.semaphore_signal(
            barrier,
            inc=1,
            device_id=(lax.rem(ctx + step, 16), head),
            device_id_type=MESH,
        )
    pl.semaphore_wait(barrier, 22)

    def near_x(step):
        return z * 4 + lax.rem(x + step, 4)

    def near_z(step):
        return lax.rem(z + step, 4) * 4 + x

    value_copies = []
    for group, (low, high) in enumerate(GROUPS):
        for number in (6, 7, 2, 3, 4, 5, 1):
            target = lax.rem(y + (0, 1, 3, 2)[number // 2], 4) * 2 + lax.rem(
                core + number % 2, 2
            )
            value_copies.append(
                copy(
                    values.at[
                        :, pl.ds(pl.multiple_of(target * FEATS + low, LANES), high - low)
                    ],
                    rows.at[y, my_rows, low:high],
                    a_send.at[group, number],
                    a_recv.at[group, number],
                    (ctx, target),
                )
            )
            value_copies[-1].start()

    first_copies = []
    for number, step in enumerate((2, 1, 3)):
        first_copies.append(
            copy(
                weight.at[0],
                all_weight.at[z, x, 0, :, own_lanes],
                w1_send.at[number],
                w1_recv.at[number],
                (near_x(step), head),
            )
        )
        first_copies.append(
            copy(
                weight.at[1],
                all_weight.at[z, x, 1, :, own_lanes],
                w1_send.at[3 + number],
                w1_recv.at[3 + number],
                (near_z(step), head),
            )
        )
    for item in first_copies:
        item.start()

    for load in loads:
        load.wait()
    spread = (
        (iota((HEADS_DEV, LANES), 1) % HEADS_DEV == iota((HEADS_DEV, LANES), 0))
        & (iota((HEADS_DEV, LANES), 1) < 100)
    ).astype(F32)
    lane_level = iota((CHUNK, LANES), 1) // HEADS_DEV
    causal = (iota((CHUNK, CHUNK), 0) >= iota((CHUNK, CHUNK), 1)) & (
        iota((CHUNK, CHUNK), 0) // 64 == iota((CHUNK, CHUNK), 1) // 64
    )
    causal_bf16 = causal.astype(F32).astype(BF16)
    causal_wide = jnp.concatenate([causal_bf16] * 3, axis=1)
    spread_bf16 = spread.astype(BF16)
    within[...] = sum(dot(part, spread_bf16, TN) for part in split3(decay[...]))
    first_half = iota((CHUNK, CHUNK), 1) < 64

    @pl.loop(0, CHUNKS)
    def _(j):
        tokens = pl.ds(pl.multiple_of(j * CHUNK, CHUNK), CHUNK)
        part = dot(causal_wide, jnp.concatenate(split3(within[tokens, :]), axis=0))
        within[tokens, :] = part
        stretch[pl.ds(j * 2, 1), :] = part[63:64, :]
        stretch[pl.ds(j * 2 + 1, 1), :] = part[127:128, :]

    sums = stretch[...]
    total_row = jnp.sum(sums, axis=0, keepdims=True)
    totals[ctx] = jnp.broadcast_to(total_row, (8, LANES))
    total_copies = []
    for step in range(1, 16):
        total_copies.append(
            copy(
                totals.at[ctx],
                totals.at[ctx],
                t_send.at[step],
                t_recv.at[step],
                (lax.rem(ctx + step, 16), head),
            )
        )
        total_copies[-1].start()

    expander[...] = (
        (iota((256, FEATS), 0) % LANES == iota((256, FEATS), 1) // WIDTH)
        .astype(F32)
        .astype(BF16)
    )

    late = iota((16, 16), 0)
    early = iota((16, 16), 1)
    small_level = iota((16, LANES), 1) // HEADS_DEV
    prefix = jnp.zeros((16, LANES), F32)
    for size, low, high in ((2, 2, 3), (4, 3, 4), (8, 4, 5), (16, 5, 9)):
        before = ((late // size == early // size) & (early < late)).astype(F32)
        prefix = jnp.where(
            (small_level >= low) & (small_level < high), exact(before, sums), prefix
        )
    stretch[...] = prefix

    block = iota((32, 16), 0)
    piece = iota((32, 16), 1)
    pick = (block < 16) & (piece == block)
    pick = pick | (
        (block >= 16) & (block < 20) & (piece // 2 == (block - 16) * 2 + 1)
    )
    pick = pick | (
        (block >= 20) & (block < 22) & (piece // 4 == (block - 20) * 2 + 1)
    )
    pick = pick | ((block == 22) & (piece >= 8))
    row_factors[...] = dot(
        split(jnp.exp(exact(pick.astype(F32), sums))), expander[...]
    )

    own_weight.wait()
    for item in first_copies:
        item.wait_recv()
    above_z = lax.rem(z + 1, 4)
    below_z = lax.rem(z + 3, 4)
    far_z = lax.rem(z + 2, 4)
    above_x = lax.rem(x + 1, 4)
    below_x = lax.rem(x + 3, 4)
    far_x = lax.rem(x + 2, 4)
    slabs = [
        lambda lanes: all_weight.at[z, :, 0, :, lanes],
        lambda lanes: all_weight.at[:, x, 1, :, lanes],
        lambda lanes: all_weight.at[below_z, :, 0, :, lanes],
        lambda lanes: all_weight.at[above_z, :, 0, :, lanes],
        lambda lanes: all_weight.at[:, below_x, 1, :, lanes],
        lambda lanes: all_weight.at[:, above_x, 1, :, lanes],
        lambda lanes: all_weight.at[far_z, 0:2, 0, :, lanes],
        lambda lanes: all_weight.at[far_z, 2:4, 0, :, lanes],
        lambda lanes: all_weight.at[0:2, far_x, 1, :, lanes],
        lambda lanes: all_weight.at[2:4, far_x, 1, :, lanes],
    ]
    second_copies = []
    forward_copies = []

    def pass_on(part, number, device):
        item = copy(part, part, w2_send.at[number], w2_recv.at[number], (device, head))
        item.start()
        second_copies.append(item)

    def arrived(number):
        part = slabs[number + 2](own_lanes)
        copy(
            part, part, w2_send.at[number], w2_recv.at[number], (near_z(1), head)
        ).wait_recv()

    def forward(number):
        part = slabs[number](own_lanes)
        item = copy(part, part, wf_send.at[number], wf_recv.at[number], (ctx, partner))
        item.start()
        forward_copies.append(item)

    pass_on(slabs[0](own_lanes), 0, near_z(1))
    pass_on(slabs[0](own_lanes), 1, near_z(3))
    pass_on(slabs[1](own_lanes), 2, near_x(1))
    pass_on(slabs[1](own_lanes), 3, near_x(3))
    forward(0)
    forward(1)

    table_rows = jnp.zeros((32, LANES), F32)
    for level in range(9):
        table_rows = table_rows + exact(
            table[level],
            jnp.where(iota((HEADS_DEV, LANES), 1) // HEADS_DEV == level, spread, 0.0),
            TN,
        )
    table_wide = jnp.concatenate(split3(table_rows), axis=0)
    class_rows = iota((32, CHUNK), 0)
    lift_lane = (lane_level == LIFT).astype(F32)
    second_row = iota((CHUNK, LANES), 0) // 64

    @pl.loop(0, CHUNKS)
    def _(j):
        tokens = pl.ds(pl.multiple_of(j * CHUNK, CHUNK), CHUNK)
        onehot = (class_rows == classes[pl.ds(j, 1), :]).astype(F32).astype(BF16)
        weights = dot(jnp.concatenate([onehot] * 3, axis=0), table_wide, TN) + lift_lane
        part = within[tokens, :]
        start = jnp.where(
            second_row == 0, stretch[pl.ds(j * 2, 1), :], stretch[pl.ds(j * 2 + 1, 1), :]
        )
        exponent = jnp.where(lane_level == LIFT, -part, part + start)
        bit = jnp.where(
            lane_level == 1,
            second_row,
            jnp.where(
                lane_level == 2,
                lax.rem(j, 2),
                jnp.where(
                    lane_level == 3,
                    lax.rem(j // 2, 2),
                    jnp.where(lane_level == 4, j // 4, 1),
                ),
            ),
        )
        every = jnp.where(bit == 1, jnp.exp(exponent) * weights, 0.0)
        for level in range(10):
            turn = (LANES - level * HEADS_DEV) % LANES
            factors[level, tokens, :] = split(pltpu.roll(every, turn, 1) if turn else every)
        incoming = entering[tokens, :]
        reader = leaving[tokens, :]
        readers[tokens, :] = jnp.concatenate([reader, reader], axis=1)
        scores = jnp.where(causal, dot(reader, incoming, NT), 0.0)
        score_high = scores.astype(BF16)
        score_low = (scores - score_high.astype(F32)).astype(BF16)
        turned = incoming.astype(F32).T
        lower = jnp.where(first_half, turned, 0.0).astype(BF16)
        upper = jnp.where(first_half, 0.0, turned).astype(BF16)
        half = jnp.concatenate([score_high, score_low, lower, upper], axis=0)
        mixers[j] = jnp.concatenate([half, half], axis=1)

    skip_row = dot(split(exact(skip[...], spread)), expander[...])

    def pair_work(pair, low, high):
        inputs = rows[pair, :, low:high].astype(F32)
        tokens = pl.ds(pl.multiple_of(pair * 256, 256), 256)
        expanded = dot(
            jnp.concatenate(
                [factors[LIFT, tokens, :], factors[0, tokens, :], factors[1, tokens, :]],
                axis=0,
            ),
            expander[:, low:high],
        )
        lifted = expanded[:256] * inputs
        states = []
        for half in range(2):
            start = half * CHUNK
            part = slice(start, start + CHUNK)
            j = pair * 2 + half
            product = dot(mixers[j], split(lifted[part], 0))
            lower_state = row_factors[pl.ds(j * 2, 1), low:high] * product[256:384]
            states.append(
                row_factors[pl.ds(j * 2 + 1, 1), low:high]
                * (lower_state + product[384:512])
            )
            gained = dot(
                readers[pl.ds(pl.multiple_of(j * CHUNK, CHUNK), CHUNK), :],
                split(lower_state, 0),
            )
            output[pair, part, low:high] = (
                expanded[256 + start : 384 + start] * (product[:128] + product[128:256])
                + expanded[512 + start : 640 + start] * gained
                + skip_row[:, low:high] * inputs[part]
            )
        pair_state[pair, :, low:high] = states[0]
        quad_state[pair, :, low:high] = (
            row_factors[pl.ds(16 + pair, 1), low:high] * states[0] + states[1]
        )

    x_copies = []
    for group, (low, high) in enumerate(GROUPS):

        @pl.loop(0, 4)
        def _(order):
            step = order + (order // 2) * (1 - 2 * lax.rem(order, 2))
            pair = lax.rem(y + 4 - step, 4)
            for half in range(2):
                place = rows.at[pair, half * CHUNK : (half + 1) * CHUNK, low:high]
                pltpu.make_async_copy(
                    place, place, a_recv.at[group, order * 2 + half]
                ).wait()
            pair_work(pair, low, high)

        for half in range(2):
            half_state[half, :, low:high] = (
                row_factors[20 + half : 21 + half, low:high]
                * quad_state[2 * half, :, low:high]
                + quad_state[2 * half + 1, :, low:high]
            )
        ring_x[x, :, low:high] = (
            row_factors[22:23, low:high] * half_state[0, :, low:high]
            + half_state[1, :, low:high]
        ).astype(BF16)
        for number, step in enumerate((2, 1, 3)):
            x_copies.append(
                copy(
                    ring_x.at[x, :, low:high],
                    ring_x.at[x, :, low:high],
                    x_send.at[group, number],
                    x_recv.at[group, number],
                    (near_x(step), head),
                )
            )
            x_copies[-1].start()
        if group == 0:
            for step in range(1, 16):
                origin = lax.rem(ctx + 16 - step, 16)
                copy(
                    totals.at[origin],
                    totals.at[origin],
                    t_send.at[step],
                    t_recv.at[step],
                    (origin, head),
                ).wait_recv()
            every_total = jnp.concatenate([totals[d][0:1, :] for d in range(16)], axis=0)
            row = iota((32, 16), 0)
            shard = iota((32, 16), 1)
            kind = row // 4
            slot = row % 4
            shard_x = shard % 4
            shard_z = shard // 4
            same_z = shard_z == z
            counted = (kind == 1) & same_z & (shard_x > slot) & (shard_x < x)
            counted = counted | ((kind == 2) & same_z & (shard_x > slot))
            counted = counted | ((kind >= 3) & (kind < 5) & same_z & (shard_x < x))
            counted = counted | ((kind == 4) & (shard_z > slot) & (shard_z < z))
            row = iota((32, LANES), 0)
            kind = row // 4
            slot = row % 4
            used = (kind == 0) & (slot == x - 1) & (lax.rem(x, 2) == 1)
            used = used | ((kind == 1) & (x >= 2) & (slot < 2))
            used = used | (kind == 2)
            used = used | ((kind == 3) & (slot == z - 1) & (lax.rem(z, 2) == 1))
            used = used | ((kind == 4) & (z >= 2) & (slot < 2))
            mix = jnp.where(used, jnp.exp(exact(counted.astype(F32), every_total)), 0.0)
            mix_factors[...] = dot(split(mix), expander[...])

    def mixed(ring, start, low, high):
        total = jnp.zeros((STATE, high - low), F32)
        for source in range(4):
            total = total + mix_factors[
                start + source : start + source + 1, low:high
            ] * ring[source, :, low:high].astype(F32)
        return total

    def hear(ring, recv, group, low, high, position, device):
        for number, step in enumerate((2, 1, 3)):
            origin = lax.rem(position + 4 - step, 4)
            copy(
                ring.at[origin, :, low:high],
                ring.at[origin, :, low:high],
                x_send.at[group, number],
                recv.at[group, number],
                (device(origin), head),
            ).wait_recv()

    def read_local(step):
        def rows_of(start, count):
            return pl.ds(pl.multiple_of(start, CHUNK), count)

        first = rows_of(step * 512 + 128, 128)
        second = rows_of(step * 512 + 384, 128)
        third = rows_of(step * 512 + 256, 256)
        fourth = rows_of(512 + step * 256, 256)
        expanded = dot(
            jnp.concatenate(
                [
                    factors[2, first, :],
                    factors[2, second, :],
                    factors[3, third, :],
                    factors[4, fourth, :],
                ],
                axis=0,
            ),
            expander[...],
        )
        upper = slice(CHUNK, 2 * CHUNK)
        output[step * 2, upper, :] += expanded[:128] * dot(
            readers[first, :], split(pair_state[step * 2], 0)
        )
        output[step * 2 + 1, upper, :] += expanded[128:256] * dot(
            readers[second, :], split(pair_state[step * 2 + 1], 0)
        )
        output[step * 2 + 1] += expanded[256:512] * dot(
            readers[third, :], split(quad_state[step * 2], 0)
        )
        output[2 + step] += expanded[512:] * dot(
            readers[fourth, :], split(half_state[0], 0)
        )

    arrived(0)
    arrived(1)
    pass_on(all_weight.at[below_z, 0:2, 0, :, own_lanes], 4, near_z(1))
    pass_on(all_weight.at[above_z, 2:4, 0, :, own_lanes], 5, near_z(3))
    forward(2)
    forward(3)

    z_copies = []
    for group, (low, high) in enumerate(GROUPS):
        hear(ring_x, x_recv, group, low, high, x, lambda origin: z * 4 + origin)
        ring_z[z, :, low:high] = mixed(ring_x, 8, low, high).astype(BF16)
        for number, step in enumerate((2, 1, 3)):
            z_copies.append(
                copy(
                    ring_z.at[z, :, low:high],
                    ring_z.at[z, :, low:high],
                    z_send.at[group, number],
                    z_recv.at[group, number],
                    (near_z(step), head),
                )
            )
            z_copies[-1].start()
        buckets[0, :, low:high] = split(mixed(ring_x, 0, low, high), 0)
        buckets[1, :, low:high] = split(mixed(ring_x, 4, low, high), 0)
        if group == 0:
            pl.loop(0, 2)(read_local)

    arrived(2)
    arrived(3)
    pass_on(all_weight.at[0:2, below_x, 1, :, own_lanes], 6, near_x(1))
    pass_on(all_weight.at[2:4, above_x, 1, :, own_lanes], 7, near_x(3))
    forward(4)
    forward(5)

    def read_levels(start, count, low):
        tokens = pl.ds(pl.multiple_of(start, CHUNK), count)
        reader = readers[tokens, :]
        expanded = dot(
            jnp.concatenate([factors[low, tokens, :], factors[low + 1, tokens, :]], axis=0),
            expander[...],
        )
        return expanded[:count] * dot(reader, buckets[0]) + expanded[count:] * dot(
            reader, buckets[1]
        )

    @pl.loop(0, 4)
    def _(pair):
        output[pair] = output[pair] + read_levels(pair * 256, 256, 5)

    for number in (4, 5, 6, 7):
        arrived(number)
        forward(number + 2)

    for group, (low, high) in enumerate(GROUPS):
        hear(ring_z, z_recv, group, low, high, z, lambda origin: origin * 4 + x)
        buckets[0, :, low:high] = split(mixed(ring_z, 12, low, high), 0)
        buckets[1, :, low:high] = split(mixed(ring_z, 16, low, high), 0)

    same_head = (
        iota((256, LANES), 0) % LANES // WIDTH == iota((256, LANES), 1) // WIDTH
    ).astype(F32).astype(BF16)

    gain_row = gain[...].reshape(1, FEATS)

    def finish(pair, side):
        here = pl.ds(pl.multiple_of(side * CHUNK, CHUNK), CHUNK)
        total = output[pair, here, :] + read_levels(pair * 256 + side * CHUNK, CHUNK, 7)
        pieces = []
        for group in range(FEATS // LANES):
            part = total[:, group * LANES : (group + 1) * LANES]
            mean_square = dot(split(part * part), same_head) * (1.0 / WIDTH)
            scaled = part * lax.rsqrt(mean_square + EPSILON)
            pieces.append(scaled * gain_row[:, group * LANES : (group + 1) * LANES])
        return jnp.concatenate(pieces, axis=1).astype(BF16)

    def place_chip(place):
        return lax.rem(y + (2, 1, 3, 0)[place], 4)

    normed_copies = []

    def hand_over(place):
        normed_send[place] = finish(place_chip(place), 1 - core)
        normed_copies.append(
            copy(
                normed_send.at[place],
                normed_all.at[place, :, own_lanes],
                n_send.at[place],
                n_recv.at[place],
                (ctx, partner),
            )
        )
        normed_copies[-1].start()

    def keep(place):
        normed_all[place, :, own_lanes] = finish(place_chip(place), core)

    hand_over(0)
    keep(0)
    hand_over(1)
    for number, slab in enumerate(slabs):
        copy(
            slab(other_lanes),
            slab(other_lanes),
            wf_send.at[number],
            wf_recv.at[number],
            (ctx, partner),
        ).wait_recv()

    up = (ctx, lax.rem(y + 1, 4) * 2 + core)
    down = (ctx, lax.rem(y + 3, 4) * 2 + core)
    partial_copies = []

    def product(first_place, last_place, quarter):
        count = last_place - first_place
        return dot(
            normed_all[first_place:last_place].reshape(count * CHUNK, 2 * FEATS),
            all_weight[quarter].reshape(TILE, 2 * FEATS),
            NT,
        )

    def send(value, place, quarter, target, send_sems, recv_sems, device):
        partial_send[place, quarter] = value.astype(BF16)
        item = copy(
            partial_send.at[place, quarter], target, send_sems, recv_sems, device
        )
        item.start()
        partial_copies.append(item)

    normed_copies[0].wait_recv()
    for quarter in (0, 2, 1, 3):
        send(
            product(0, 1, quarter),
            0,
            quarter,
            relay_recv.at[quarter],
            r_send.at[quarter],
            r_recv.at[quarter],
            up if quarter < 2 else down,
        )
    keep(1)
    hand_over(2)
    keep(2)
    normed_copies[1].wait_recv()
    normed_copies[2].wait_recv()

    def send_near(value, place, quarter):
        send(
            value,
            place,
            quarter,
            partial_recv.at[place - 1, quarter],
            p_send.at[place - 1, quarter],
            p_recv.at[place - 1, quarter],
            up if place == 1 else down,
        )

    for quarter in (2, 0, 3, 1):
        both = product(1, 3, quarter)
        if quarter < 2:
            held[quarter] = both[:CHUNK]
            send_near(both[CHUNK:], 2, quarter)
        else:
            send_near(both[:CHUNK], 1, quarter)
            held[quarter] = both[CHUNK:]
    hand_over(3)
    keep(3)
    for quarter in (0, 2, 1, 3):
        partial_copies[(0, 2, 1, 3).index(quarter)].wait_recv()
        send_near(
            held[quarter] + relay_recv[quarter].astype(F32),
            1 if quarter < 2 else 2,
            quarter,
        )
    normed_copies[3].wait_recv()
    for quarter in range(4):
        own_sum[:, quarter * TILE : (quarter + 1) * TILE] = product(3, 4, quarter)
    for quarter in range(4):
        for place in range(2):
            copy(
                partial_recv.at[place, quarter],
                partial_recv.at[place, quarter],
                p_send.at[place, quarter],
                p_recv.at[place, quarter],
                up,
            ).wait_recv()
        columns = slice(quarter * TILE, (quarter + 1) * TILE)
        result[:, columns] = (
            own_sum[:, columns]
            + partial_recv[0, quarter].astype(F32)
            + partial_recv[1, quarter].astype(F32)
        ).astype(BF16)

    for item in (
        value_copies
        + first_copies
        + total_copies
        + second_copies
        + forward_copies
        + x_copies
        + z_copies
        + normed_copies
        + partial_copies
    ):
        item.wait_send()


def on_device(
    values,
    state_in,
    state_out,
    log_decay,
    level_class,
    level_table,
    skip_gain,
    norm_gain,
    out_weight,
):
    columns = out_weight.shape[1]
    weight = out_weight.T.reshape(2, columns // 2, FEATS)
    anywhere = pl.BlockSpec(memory_space=pl.ANY)
    dma = pltpu.SemaphoreType.DMA
    groups = len(GROUPS)
    return pl.pallas_call(
        kernel,
        out_shape=jax.ShapeDtypeStruct((CHUNK, OUTS), BF16),
        in_specs=[anywhere] * 9,
        out_specs=pl.BlockSpec(memory_space=pltpu.VMEM),
        scratch_shapes=[
            pltpu.VMEM((4, 2 * CHUNK, FEATS), BF16),
            pltpu.VMEM((CHUNKS * CHUNK, STATE), BF16),
            pltpu.VMEM((CHUNKS * CHUNK, STATE), BF16),
            pltpu.VMEM((HEADS_DEV, CHUNKS * CHUNK), F32),
            pltpu.VMEM((CHUNKS, CHUNK), jnp.int32),
            pltpu.VMEM((9, HEADS_DEV, 32), F32),
            pltpu.VMEM((1, HEADS_DEV), F32),
            pltpu.VMEM((FEATS,), F32),
            pltpu.VMEM((4, 4, 2, 80, 2 * FEATS), BF16),
            pltpu.VMEM((256, FEATS), BF16),
            pltpu.VMEM((CHUNKS * CHUNK, LANES), F32),
            pltpu.VMEM((16, LANES), F32),
            pltpu.VMEM((10, CHUNKS * CHUNK, 2 * LANES), BF16),
            pltpu.VMEM((CHUNKS, 4 * CHUNK, 2 * STATE), BF16),
            pltpu.VMEM((CHUNKS * CHUNK, 2 * STATE), BF16),
            pltpu.VMEM((16, 8, LANES), F32),
            pltpu.VMEM((32, FEATS), F32),
            pltpu.VMEM((32, FEATS), F32),
            pltpu.VMEM((4, STATE, FEATS), F32),
            pltpu.VMEM((4, STATE, FEATS), F32),
            pltpu.VMEM((2, STATE, FEATS), F32),
            pltpu.VMEM((4, 2 * CHUNK, FEATS), F32),
            pltpu.VMEM((4, STATE, FEATS), BF16),
            pltpu.VMEM((4, STATE, FEATS), BF16),
            pltpu.VMEM((2, 2 * STATE, FEATS), BF16),
            pltpu.VMEM((4, CHUNK, FEATS), BF16),
            pltpu.VMEM((4, CHUNK, 2 * FEATS), BF16),
            pltpu.VMEM((CHUNK, OUTS), F32),
            pltpu.VMEM((4, CHUNK, TILE), F32),
            pltpu.VMEM((3, 4, CHUNK, TILE), BF16),
            pltpu.VMEM((4, CHUNK, TILE), BF16),
            pltpu.VMEM((2, 4, CHUNK, TILE), BF16),
            dma((8,)),
            dma((groups, 8)),
            dma((groups, 8)),
            dma((6,)),
            dma((6,)),
            dma((8,)),
            dma((8,)),
            dma((10,)),
            dma((10,)),
            dma((16,)),
            dma((16,)),
            dma((groups, 3)),
            dma((groups, 3)),
            dma((groups, 3)),
            dma((groups, 3)),
            dma((4,)),
            dma((4,)),
            dma((4,)),
            dma((4,)),
            dma((2, 4)),
            dma((2, 4)),
        ],
        compiler_params=pltpu.CompilerParams(
            collective_id=0,
            has_side_effects=True,
            vmem_limit_bytes=60 * 1024 * 1024,
        ),
        name="layer",
    )(
        values,
        state_in,
        state_out,
        log_decay.T,
        level_class.reshape(CHUNKS, CHUNK),
        level_table.transpose(1, 2, 0),
        skip_gain.reshape(1, -1),
        norm_gain,
        weight,
    )


def solution(mesh):
    return jax.shard_map(
        on_device,
        mesh=mesh,
        in_specs=(
            P(("ctx", "head"), None),
            P("ctx", None),
            P("ctx", None),
            P("ctx", "head"),
            P("ctx"),
            P(None, None, "head"),
            P("head"),
            P("head"),
            P("head", "ctx"),
        ),
        out_specs=P(("ctx", "head"), None),
        check_vma=False,
    )
```

```python
import jax
import jax.numpy as jnp
from jax import lax
from jax.experimental import pallas as pl
from jax.experimental.pallas import tpu as pltpu
from jax.sharding import PartitionSpec as P

MESH = pl.DeviceIdType.MESH
PRECISE = lax.Precision.HIGHEST
EPSILON = 1e-05
F32 = jnp.float32
BF16 = jnp.bfloat16
LANES = 128
HEADS_DEV = 10
WIDTH = 64
FEATS = HEADS_DEV * WIDTH
STATE = 128
CHUNK = 128
CHUNKS = 8
OUTS = 2560
LIFT = 9
GROUPS = ((0, 384), (384, 640))
TILE = OUTS // 4

NT = (((1,), (1,)), ((), ()))
TN = (((0,), (0,)), ((), ()))
NN = (((1,), (0,)), ((), ()))


def iota(shape, axis):
    return lax.broadcasted_iota(jnp.int32, shape, axis)


def dot(a, b, dims=NN):
    return lax.dot_general(a, b, dims, preferred_element_type=F32)


def exact(a, b, dims=NN):
    return lax.dot_general(a, b, dims, precision=PRECISE, preferred_element_type=F32)


def split(value, axis=1):
    high = value.astype(BF16)
    low = (value - high.astype(F32)).astype(BF16)
    return jnp.concatenate([high, low], axis=axis)


def split3(value):
    high = value.astype(BF16)
    rest = value - high.astype(F32)
    middle = rest.astype(BF16)
    return high, middle, (rest - middle.astype(F32)).astype(BF16)


def kernel(
    values,
    state_in,
    state_out,
    log_decay,
    level_class,
    level_table,
    skip_gain,
    norm_gain,
    weight,
    result,
    rows,
    entering,
    leaving,
    decay,
    classes,
    table,
    skip,
    gain,
    all_weight,
    expander,
    within,
    stretch,
    factors,
    mixers,
    readers,
    totals,
    row_factors,
    mix_factors,
    pair_state,
    quad_state,
    half_state,
    output,
    ring_x,
    ring_z,
    buckets,
    normed_send,
    normed_all,
    own_sum,
    held,
    partial_send,
    relay_recv,
    partial_recv,
    local_sem,
    a_send,
    a_recv,
    w1_send,
    w1_recv,
    w2_send,
    w2_recv,
    wf_send,
    wf_recv,
    t_send,
    t_recv,
    x_send,
    x_recv,
    z_send,
    z_recv,
    n_send,
    n_recv,
    r_send,
    r_recv,
    p_send,
    p_recv,
):
    ctx = lax.axis_index("ctx")
    head = lax.axis_index("head")
    x = lax.rem(ctx, 4)
    z = ctx // 4
    y = head // 2
    core = lax.rem(head, 2)
    partner = y * 2 + (1 - core)

    def copy(source, target, send, recv, device):
        return pltpu.make_async_remote_copy(
            src_ref=source,
            dst_ref=target,
            send_sem=send,
            recv_sem=recv,
            device_id=device,
            device_id_type=MESH,
        )

    loads = [
        pltpu.make_async_copy(source, target, local_sem.at[number])
        for number, (source, target) in enumerate(
            [
                (log_decay, decay),
                (level_class, classes),
                (level_table, table),
                (state_in, entering),
                (state_out, leaving),
                (skip_gain, skip),
                (norm_gain, gain),
            ]
        )
    ]
    for load in loads:
        load.start()
    own_lanes = pl.ds(pl.multiple_of(core * FEATS, LANES), FEATS)
    other_lanes = pl.ds(pl.multiple_of((1 - core) * FEATS, LANES), FEATS)
    my_rows = pl.ds(pl.multiple_of(core * CHUNK, CHUNK), CHUNK)
    for group, (low, high) in enumerate(GROUPS):
        pltpu.make_async_copy(
            values.at[:, pl.ds(pl.multiple_of(head * FEATS + low, LANES), high - low)],
            rows.at[y, my_rows, low:high],
            a_recv.at[group, 0],
        ).start()
    own_weight = pltpu.make_async_copy(
        weight, all_weight.at[z, x, :, :, own_lanes], local_sem.at[7]
    )
    own_weight.start()

    barrier = pltpu.get_barrier_semaphore()
    for step in range(1, 8):
        pl.semaphore_signal(
            barrier,
            inc=1,
            device_id=(ctx, lax.rem(head + step, 8)),
            device_id_type=MESH,
        )
    def near_x(step):
        return z * 4 + lax.rem(x + step, 4)

    def near_z(step):
        return lax.rem(z + step, 4) * 4 + x

    for step in range(1, 4):
        for device in (near_x(step), near_z(step)):
            pl.semaphore_signal(
                barrier, inc=1, device_id=(device, head), device_id_type=MESH
            )
    pl.semaphore_wait(barrier, 13)

    value_copies = []
    for group, (low, high) in enumerate(GROUPS):
        for number in (6, 7, 2, 3, 4, 5, 1):
            target = lax.rem(y + (0, 1, 3, 2)[number // 2], 4) * 2 + lax.rem(
                core + number % 2, 2
            )
            value_copies.append(
                copy(
                    values.at[
                        :, pl.ds(pl.multiple_of(target * FEATS + low, LANES), high - low)
                    ],
                    rows.at[y, my_rows, low:high],
                    a_send.at[group, number],
                    a_recv.at[group, number],
                    (ctx, target),
                )
            )
            value_copies[-1].start()

    first_copies = []
    for number, step in enumerate((2, 1, 3)):
        first_copies.append(
            copy(
                weight.at[0],
                all_weight.at[z, x, 0, :, own_lanes],
                w1_send.at[number],
                w1_recv.at[number],
                (near_x(step), head),
            )
        )
        first_copies.append(
            copy(
                weight.at[1],
                all_weight.at[z, x, 1, :, own_lanes],
                w1_send.at[3 + number],
                w1_recv.at[3 + number],
                (near_z(step), head),
            )
        )
    for item in first_copies:
        item.start()

    for load in loads:
        load.wait()
    spread = (
        (iota((HEADS_DEV, LANES), 1) % HEADS_DEV == iota((HEADS_DEV, LANES), 0))
        & (iota((HEADS_DEV, LANES), 1) < 100)
    ).astype(F32)
    lane_level = iota((CHUNK, LANES), 1) // HEADS_DEV
    causal = (iota((CHUNK, CHUNK), 0) >= iota((CHUNK, CHUNK), 1)) & (
        iota((CHUNK, CHUNK), 0) // 64 == iota((CHUNK, CHUNK), 1) // 64
    )
    causal_bf16 = causal.astype(F32).astype(BF16)
    causal_wide = jnp.concatenate([causal_bf16] * 3, axis=1)
    spread_bf16 = spread.astype(BF16)
    within[...] = sum(dot(part, spread_bf16, TN) for part in split3(decay[...]))
    first_half = iota((CHUNK, CHUNK), 1) < 64

    @pl.loop(0, CHUNKS)
    def _(j):
        tokens = pl.ds(pl.multiple_of(j * CHUNK, CHUNK), CHUNK)
        part = dot(causal_wide, jnp.concatenate(split3(within[tokens, :]), axis=0))
        within[tokens, :] = part
        stretch[pl.ds(j * 2, 1), :] = part[63:64, :]
        stretch[pl.ds(j * 2 + 1, 1), :] = part[127:128, :]

    sums = stretch[...]
    total_row = jnp.sum(sums, axis=0, keepdims=True)
    totals[z, x] = jnp.broadcast_to(total_row, (8, LANES))
    total_copies = []

    def share_totals(part, first, device):
        for step in range(1, 4):
            item = copy(
                part,
                part,
                t_send.at[first + step],
                t_recv.at[first + step],
                (device(step), head),
            )
            item.start()
            total_copies.append(item)

    def hear_totals(part, first):
        for step in range(1, 4):
            piece = part(step)
            copy(
                piece,
                piece,
                t_send.at[first + step],
                t_recv.at[first + step],
                (near_x(1), head),
            ).wait_recv()

    share_totals(totals.at[z, x], 0, near_x)

    expander[...] = (
        (iota((256, FEATS), 0) % LANES == iota((256, FEATS), 1) // WIDTH)
        .astype(F32)
        .astype(BF16)
    )

    late = iota((16, 16), 0)
    early = iota((16, 16), 1)
    small_level = iota((16, LANES), 1) // HEADS_DEV
    prefix = jnp.zeros((16, LANES), F32)
    for size, low, high in ((2, 2, 3), (4, 3, 4), (8, 4, 5), (16, 5, 9)):
        before = ((late // size == early // size) & (early < late)).astype(F32)
        prefix = jnp.where(
            (small_level >= low) & (small_level < high), exact(before, sums), prefix
        )
    stretch[...] = prefix

    block = iota((32, 16), 0)
    piece = iota((32, 16), 1)
    pick = (block < 16) & (piece == block)
    pick = pick | (
        (block >= 16) & (block < 20) & (piece // 2 == (block - 16) * 2 + 1)
    )
    pick = pick | (
        (block >= 20) & (block < 22) & (piece // 4 == (block - 20) * 2 + 1)
    )
    pick = pick | ((block == 22) & (piece >= 8))
    row_factors[...] = dot(
        split(jnp.exp(exact(pick.astype(F32), sums))), expander[...]
    )

    table_rows = jnp.zeros((32, LANES), F32)
    for level in range(9):
        table_rows = table_rows + exact(
            table[level],
            jnp.where(iota((HEADS_DEV, LANES), 1) // HEADS_DEV == level, spread, 0.0),
            TN,
        )
    table_wide = jnp.concatenate(split3(table_rows), axis=0)
    class_rows = iota((32, CHUNK), 0)
    lift_lane = (lane_level == LIFT).astype(F32)
    second_row = iota((CHUNK, LANES), 0) // 64

    @pl.loop(0, CHUNKS)
    def _(j):
        tokens = pl.ds(pl.multiple_of(j * CHUNK, CHUNK), CHUNK)
        onehot = (class_rows == classes[pl.ds(j, 1), :]).astype(F32).astype(BF16)
        weights = dot(jnp.concatenate([onehot] * 3, axis=0), table_wide, TN) + lift_lane
        part = within[tokens, :]
        start = jnp.where(
            second_row == 0, stretch[pl.ds(j * 2, 1), :], stretch[pl.ds(j * 2 + 1, 1), :]
        )
        exponent = jnp.where(lane_level == LIFT, -part, part + start)
        bit = jnp.where(
            lane_level == 1,
            second_row,
            jnp.where(
                lane_level == 2,
                lax.rem(j, 2),
                jnp.where(
                    lane_level == 3,
                    lax.rem(j // 2, 2),
                    jnp.where(lane_level == 4, j // 4, 1),
                ),
            ),
        )
        every = jnp.where(bit == 1, jnp.exp(exponent) * weights, 0.0)
        for level in range(10):
            turn = (LANES - level * HEADS_DEV) % LANES
            factors[level, tokens, :] = split(pltpu.roll(every, turn, 1) if turn else every)
        incoming = entering[tokens, :]
        reader = leaving[tokens, :]
        readers[tokens, :] = jnp.concatenate([reader, reader], axis=1)
        scores = jnp.where(causal, dot(reader, incoming, NT), 0.0)
        score_high = scores.astype(BF16)
        score_low = (scores - score_high.astype(F32)).astype(BF16)
        turned = incoming.astype(F32).T
        lower = jnp.where(first_half, turned, 0.0).astype(BF16)
        upper = jnp.where(first_half, 0.0, turned).astype(BF16)
        half = jnp.concatenate([score_high, score_low, lower, upper], axis=0)
        mixers[j] = jnp.concatenate([half, half], axis=1)

    skip_row = dot(split(exact(skip[...], spread)), expander[...])

    hear_totals(lambda step: totals.at[z, lax.rem(x + 4 - step, 4)], 0)
    share_totals(totals.at[z], 4, near_z)

    own_weight.wait()
    for item in first_copies:
        item.wait_recv()
    above_z = lax.rem(z + 1, 4)
    below_z = lax.rem(z + 3, 4)
    far_z = lax.rem(z + 2, 4)
    above_x = lax.rem(x + 1, 4)
    below_x = lax.rem(x + 3, 4)
    far_x = lax.rem(x + 2, 4)
    slabs = [
        lambda lanes: all_weight.at[z, :, 0, :, lanes],
        lambda lanes: all_weight.at[:, x, 1, :, lanes],
        lambda lanes: all_weight.at[below_z, :, 0, :, lanes],
        lambda lanes: all_weight.at[above_z, :, 0, :, lanes],
        lambda lanes: all_weight.at[:, below_x, 1, :, lanes],
        lambda lanes: all_weight.at[:, above_x, 1, :, lanes],
        lambda lanes: all_weight.at[far_z, 0:2, 0, :, lanes],
        lambda lanes: all_weight.at[far_z, 2:4, 0, :, lanes],
        lambda lanes: all_weight.at[0:2, far_x, 1, :, lanes],
        lambda lanes: all_weight.at[2:4, far_x, 1, :, lanes],
    ]
    second_copies = []
    forward_copies = []

    def pass_on(part, number, device):
        item = copy(part, part, w2_send.at[number], w2_recv.at[number], (device, head))
        item.start()
        second_copies.append(item)

    def arrived(number):
        part = slabs[number + 2](own_lanes)
        copy(
            part, part, w2_send.at[number], w2_recv.at[number], (near_z(1), head)
        ).wait_recv()

    def forward(number):
        part = slabs[number](own_lanes)
        item = copy(part, part, wf_send.at[number], wf_recv.at[number], (ctx, partner))
        item.start()
        forward_copies.append(item)

    pass_on(slabs[0](own_lanes), 0, near_z(1))
    pass_on(slabs[0](own_lanes), 1, near_z(3))
    pass_on(slabs[1](own_lanes), 2, near_x(1))
    pass_on(slabs[1](own_lanes), 3, near_x(3))
    forward(0)
    forward(1)

    def pair_work(pair, low, high):
        inputs = rows[pair, :, low:high].astype(F32)
        tokens = pl.ds(pl.multiple_of(pair * 256, 256), 256)
        expanded = dot(
            jnp.concatenate(
                [factors[LIFT, tokens, :], factors[0, tokens, :], factors[1, tokens, :]],
                axis=0,
            ),
            expander[:, low:high],
        )
        lifted = expanded[:256] * inputs
        states = []
        for half in range(2):
            start = half * CHUNK
            part = slice(start, start + CHUNK)
            j = pair * 2 + half
            product = dot(mixers[j], split(lifted[part], 0))
            lower_state = row_factors[pl.ds(j * 2, 1), :][:, low:high] * product[256:384]
            states.append(
                row_factors[pl.ds(j * 2 + 1, 1), :][:, low:high]
                * (lower_state + product[384:512])
            )
            gained = dot(
                readers[pl.ds(pl.multiple_of(j * CHUNK, CHUNK), CHUNK), :],
                split(lower_state, 0),
            )
            output[pair, part, low:high] = (
                expanded[256 + start : 384 + start] * (product[:128] + product[128:256])
                + expanded[512 + start : 640 + start] * gained
                + skip_row[:, low:high] * inputs[part]
            )
        pair_state[pair, :, low:high] = states[0]
        quad_state[pair, :, low:high] = (
            row_factors[pl.ds(16 + pair, 1), :][:, low:high] * states[0] + states[1]
        )

    x_copies = []
    for group, (low, high) in enumerate(GROUPS):

        @pl.loop(0, 4)
        def _(order):
            step = order + (order // 2) * (1 - 2 * lax.rem(order, 2))
            pair = lax.rem(y + 4 - step, 4)
            for half in range(2):
                place = rows.at[pair, half * CHUNK : (half + 1) * CHUNK, low:high]
                pltpu.make_async_copy(
                    place, place, a_recv.at[group, order * 2 + half]
                ).wait()
            pair_work(pair, low, high)

        for half in range(2):
            half_state[half, :, low:high] = (
                row_factors[20 + half : 21 + half, low:high]
                * quad_state[2 * half, :, low:high]
                + quad_state[2 * half + 1, :, low:high]
            )
        ring_x[x, :, low:high] = (
            row_factors[22:23, low:high] * half_state[0, :, low:high]
            + half_state[1, :, low:high]
        ).astype(BF16)
        for number, step in enumerate((2, 1, 3)):
            x_copies.append(
                copy(
                    ring_x.at[x, :, low:high],
                    ring_x.at[x, :, low:high],
                    x_send.at[group, number],
                    x_recv.at[group, number],
                    (near_x(step), head),
                )
            )
            x_copies[-1].start()
        if group == 0:
            hear_totals(lambda step: totals.at[lax.rem(z + 4 - step, 4)], 4)
            every_total = jnp.concatenate(
                [totals[d // 4, d % 4][0:1, :] for d in range(16)], axis=0
            )
            row = iota((32, 16), 0)
            shard = iota((32, 16), 1)
            kind = row // 4
            slot = row % 4
            shard_x = shard % 4
            shard_z = shard // 4
            same_z = shard_z == z
            counted = (kind == 1) & same_z & (shard_x > slot) & (shard_x < x)
            counted = counted | ((kind == 2) & same_z & (shard_x > slot))
            counted = counted | ((kind >= 3) & (kind < 5) & same_z & (shard_x < x))
            counted = counted | ((kind == 4) & (shard_z > slot) & (shard_z < z))
            row = iota((32, LANES), 0)
            kind = row // 4
            slot = row % 4
            used = (kind == 0) & (slot == x - 1) & (lax.rem(x, 2) == 1)
            used = used | ((kind == 1) & (x >= 2) & (slot < 2))
            used = used | (kind == 2)
            used = used | ((kind == 3) & (slot == z - 1) & (lax.rem(z, 2) == 1))
            used = used | ((kind == 4) & (z >= 2) & (slot < 2))
            mix = jnp.where(used, jnp.exp(exact(counted.astype(F32), every_total)), 0.0)
            mix_factors[...] = dot(split(mix), expander[...])

    def mixed(ring, start, low, high):
        total = jnp.zeros((STATE, high - low), F32)
        for source in range(4):
            total = total + mix_factors[
                start + source : start + source + 1, low:high
            ] * ring[source, :, low:high].astype(F32)
        return total

    def hear(ring, recv, group, low, high, position, device):
        for number, step in enumerate((2, 1, 3)):
            origin = lax.rem(position + 4 - step, 4)
            copy(
                ring.at[origin, :, low:high],
                ring.at[origin, :, low:high],
                x_send.at[group, number],
                recv.at[group, number],
                (device(origin), head),
            ).wait_recv()

    def read_local(step):
        def rows_of(start, count):
            return pl.ds(pl.multiple_of(start, CHUNK), count)

        first = rows_of(step * 512 + 128, 128)
        second = rows_of(step * 512 + 384, 128)
        third = rows_of(step * 512 + 256, 256)
        fourth = rows_of(512 + step * 256, 256)
        expanded = dot(
            jnp.concatenate(
                [
                    factors[2, first, :],
                    factors[2, second, :],
                    factors[3, third, :],
                    factors[4, fourth, :],
                ],
                axis=0,
            ),
            expander[...],
        )
        upper = slice(CHUNK, 2 * CHUNK)
        output[step * 2, upper, :] += expanded[:128] * dot(
            readers[first, :], split(pair_state[step * 2], 0)
        )
        output[step * 2 + 1, upper, :] += expanded[128:256] * dot(
            readers[second, :], split(pair_state[step * 2 + 1], 0)
        )
        output[step * 2 + 1] += expanded[256:512] * dot(
            readers[third, :], split(quad_state[step * 2], 0)
        )
        output[2 + step] += expanded[512:] * dot(
            readers[fourth, :], split(half_state[0], 0)
        )

    arrived(0)
    arrived(1)
    pass_on(all_weight.at[below_z, 0:2, 0, :, own_lanes], 4, near_z(1))
    pass_on(all_weight.at[above_z, 2:4, 0, :, own_lanes], 5, near_z(3))
    forward(2)
    forward(3)
    pl.loop(0, 2)(read_local)

    z_copies = []
    for group, (low, high) in enumerate(GROUPS):
        hear(ring_x, x_recv, group, low, high, x, lambda origin: z * 4 + origin)
        ring_z[z, :, low:high] = mixed(ring_x, 8, low, high).astype(BF16)
        for number, step in enumerate((2, 1, 3)):
            z_copies.append(
                copy(
                    ring_z.at[z, :, low:high],
                    ring_z.at[z, :, low:high],
                    z_send.at[group, number],
                    z_recv.at[group, number],
                    (near_z(step), head),
                )
            )
            z_copies[-1].start()
        buckets[0, :, low:high] = split(mixed(ring_x, 0, low, high), 0)
        buckets[1, :, low:high] = split(mixed(ring_x, 4, low, high), 0)

    arrived(2)
    arrived(3)
    pass_on(all_weight.at[0:2, below_x, 1, :, own_lanes], 6, near_x(1))
    pass_on(all_weight.at[2:4, above_x, 1, :, own_lanes], 7, near_x(3))
    forward(4)
    forward(5)

    def read_levels(start, count, low):
        tokens = pl.ds(pl.multiple_of(start, CHUNK), count)
        reader = readers[tokens, :]
        expanded = dot(
            jnp.concatenate([factors[low, tokens, :], factors[low + 1, tokens, :]], axis=0),
            expander[...],
        )
        return expanded[:count] * dot(reader, buckets[0]) + expanded[count:] * dot(
            reader, buckets[1]
        )

    @pl.loop(0, 4)
    def _(pair):
        output[pair] = output[pair] + read_levels(pair * 256, 256, 5)

    for number in (4, 5, 6, 7):
        arrived(number)
        forward(number + 2)

    for group, (low, high) in enumerate(GROUPS):
        hear(ring_z, z_recv, group, low, high, z, lambda origin: origin * 4 + x)
        buckets[0, :, low:high] = split(mixed(ring_z, 12, low, high), 0)
        buckets[1, :, low:high] = split(mixed(ring_z, 16, low, high), 0)

    same_head = (
        iota((256, LANES), 0) % LANES // WIDTH == iota((256, LANES), 1) // WIDTH
    ).astype(F32).astype(BF16)

    gain_row = gain[...].reshape(1, FEATS)

    def finish(pair, side):
        here = pl.ds(pl.multiple_of(side * CHUNK, CHUNK), CHUNK)
        total = output[pair, here, :] + read_levels(pair * 256 + side * CHUNK, CHUNK, 7)
        pieces = []
        for group in range(FEATS // LANES):
            part = total[:, group * LANES : (group + 1) * LANES]
            mean_square = dot(split(part * part), same_head) * (1.0 / WIDTH)
            scaled = part * lax.rsqrt(mean_square + EPSILON)
            pieces.append(scaled * gain_row[:, group * LANES : (group + 1) * LANES])
        return jnp.concatenate(pieces, axis=1).astype(BF16)

    def place_chip(place):
        return lax.rem(y + (2, 1, 3, 0)[place], 4)

    normed_copies = []

    def hand_over(place):
        normed_send[place] = finish(place_chip(place), 1 - core)
        normed_copies.append(
            copy(
                normed_send.at[place],
                normed_all.at[place, :, own_lanes],
                n_send.at[place],
                n_recv.at[place],
                (ctx, partner),
            )
        )
        normed_copies[-1].start()

    def keep(place):
        normed_all[place, :, own_lanes] = finish(place_chip(place), core)

    hand_over(0)
    keep(0)
    hand_over(1)
    for number, slab in enumerate(slabs):
        copy(
            slab(other_lanes),
            slab(other_lanes),
            wf_send.at[number],
            wf_recv.at[number],
            (ctx, partner),
        ).wait_recv()

    up = (ctx, lax.rem(y + 1, 4) * 2 + core)
    down = (ctx, lax.rem(y + 3, 4) * 2 + core)
    partial_copies = []

    def product(first_place, last_place, quarter):
        count = last_place - first_place
        return dot(
            normed_all[first_place:last_place].reshape(count * CHUNK, 2 * FEATS),
            all_weight[quarter].reshape(TILE, 2 * FEATS),
            NT,
        )

    def send(value, place, quarter, target, send_sems, recv_sems, device):
        partial_send[place, quarter] = value.astype(BF16)
        item = copy(
            partial_send.at[place, quarter], target, send_sems, recv_sems, device
        )
        item.start()
        partial_copies.append(item)

    normed_copies[0].wait_recv()
    for quarter in (0, 2, 1, 3):
        send(
            product(0, 1, quarter),
            0,
            quarter,
            relay_recv.at[quarter],
            r_send.at[quarter],
            r_recv.at[quarter],
            up if quarter < 2 else down,
        )
    keep(1)
    hand_over(2)
    keep(2)
    normed_copies[1].wait_recv()
    normed_copies[2].wait_recv()

    def send_near(value, place, quarter):
        send(
            value,
            place,
            quarter,
            partial_recv.at[place - 1, quarter],
            p_send.at[place - 1, quarter],
            p_recv.at[place - 1, quarter],
            up if place == 1 else down,
        )

    for quarter in (2, 0, 3, 1):
        both = product(1, 3, quarter)
        if quarter < 2:
            held[quarter] = both[:CHUNK]
            send_near(both[CHUNK:], 2, quarter)
        else:
            send_near(both[:CHUNK], 1, quarter)
            held[quarter] = both[CHUNK:]
    hand_over(3)
    keep(3)
    for quarter in (0, 2, 1, 3):
        partial_copies[(0, 2, 1, 3).index(quarter)].wait_recv()
        send_near(
            held[quarter] + relay_recv[quarter].astype(F32),
            1 if quarter < 2 else 2,
            quarter,
        )
    normed_copies[3].wait_recv()
    for quarter in range(4):
        own_sum[:, quarter * TILE : (quarter + 1) * TILE] = product(3, 4, quarter)
    for quarter in range(4):
        for place in range(2):
            copy(
                partial_recv.at[place, quarter],
                partial_recv.at[place, quarter],
                p_send.at[place, quarter],
                p_recv.at[place, quarter],
                up,
            ).wait_recv()
        columns = slice(quarter * TILE, (quarter + 1) * TILE)
        result[:, columns] = (
            own_sum[:, columns]
            + partial_recv[0, quarter].astype(F32)
            + partial_recv[1, quarter].astype(F32)
        ).astype(BF16)

    for item in (
        value_copies
        + first_copies
        + total_copies
        + second_copies
        + forward_copies
        + x_copies
        + z_copies
        + normed_copies
        + partial_copies
    ):
        item.wait_send()


def on_device(
    values,
    state_in,
    state_out,
    log_decay,
    level_class,
    level_table,
    skip_gain,
    norm_gain,
    out_weight,
):
    columns = out_weight.shape[1]
    weight = out_weight.T.reshape(2, columns // 2, FEATS)
    anywhere = pl.BlockSpec(memory_space=pl.ANY)
    dma = pltpu.SemaphoreType.DMA
    groups = len(GROUPS)
    return pl.pallas_call(
        kernel,
        out_shape=jax.ShapeDtypeStruct((CHUNK, OUTS), BF16),
        in_specs=[anywhere] * 9,
        out_specs=pl.BlockSpec(memory_space=pltpu.VMEM),
        scratch_shapes=[
            pltpu.VMEM((4, 2 * CHUNK, FEATS), BF16),
            pltpu.VMEM((CHUNKS * CHUNK, STATE), BF16),
            pltpu.VMEM((CHUNKS * CHUNK, STATE), BF16),
            pltpu.VMEM((HEADS_DEV, CHUNKS * CHUNK), F32),
            pltpu.VMEM((CHUNKS, CHUNK), jnp.int32),
            pltpu.VMEM((9, HEADS_DEV, 32), F32),
            pltpu.VMEM((1, HEADS_DEV), F32),
            pltpu.VMEM((FEATS,), F32),
            pltpu.VMEM((4, 4, 2, 80, 2 * FEATS), BF16),
            pltpu.VMEM((256, FEATS), BF16),
            pltpu.VMEM((CHUNKS * CHUNK, LANES), F32),
            pltpu.VMEM((16, LANES), F32),
            pltpu.VMEM((10, CHUNKS * CHUNK, 2 * LANES), BF16),
            pltpu.VMEM((CHUNKS, 4 * CHUNK, 2 * STATE), BF16),
            pltpu.VMEM((CHUNKS * CHUNK, 2 * STATE), BF16),
            pltpu.VMEM((4, 4, 8, LANES), F32),
            pltpu.VMEM((32, FEATS), F32),
            pltpu.VMEM((32, FEATS), F32),
            pltpu.VMEM((4, STATE, FEATS), F32),
            pltpu.VMEM((4, STATE, FEATS), F32),
            pltpu.VMEM((2, STATE, FEATS), F32),
            pltpu.VMEM((4, 2 * CHUNK, FEATS), F32),
            pltpu.VMEM((4, STATE, FEATS), BF16),
            pltpu.VMEM((4, STATE, FEATS), BF16),
            pltpu.VMEM((2, 2 * STATE, FEATS), BF16),
            pltpu.VMEM((4, CHUNK, FEATS), BF16),
            pltpu.VMEM((4, CHUNK, 2 * FEATS), BF16),
            pltpu.VMEM((CHUNK, OUTS), F32),
            pltpu.VMEM((4, CHUNK, TILE), F32),
            pltpu.VMEM((3, 4, CHUNK, TILE), BF16),
            pltpu.VMEM((4, CHUNK, TILE), BF16),
            pltpu.VMEM((2, 4, CHUNK, TILE), BF16),
            dma((8,)),
            dma((groups, 8)),
            dma((groups, 8)),
            dma((6,)),
            dma((6,)),
            dma((8,)),
            dma((8,)),
            dma((10,)),
            dma((10,)),
            dma((8,)),
            dma((8,)),
            dma((groups, 3)),
            dma((groups, 3)),
            dma((groups, 3)),
            dma((groups, 3)),
            dma((4,)),
            dma((4,)),
            dma((4,)),
            dma((4,)),
            dma((2, 4)),
            dma((2, 4)),
        ],
        compiler_params=pltpu.CompilerParams(
            collective_id=0,
            has_side_effects=True,
            vmem_limit_bytes=60 * 1024 * 1024,
        ),
        name="layer",
    )(
        values,
        state_in,
        state_out,
        log_decay.T,
        level_class.reshape(CHUNKS, CHUNK),
        level_table.transpose(1, 2, 0),
        skip_gain.reshape(1, -1),
        norm_gain,
        weight,
    )


def solution(mesh):
    return jax.shard_map(
        on_device,
        mesh=mesh,
        in_specs=(
            P(("ctx", "head"), None),
            P("ctx", None),
            P("ctx", None),
            P("ctx", "head"),
            P("ctx"),
            P(None, None, "head"),
            P("head"),
            P("head"),
            P("head", "ctx"),
        ),
        out_specs=P(("ctx", "head"), None),
        check_vma=False,
    )
```

```python
import jax
import jax.numpy as jnp
from jax import lax
from jax.experimental import pallas as pl
from jax.experimental.pallas import tpu as pltpu
from jax.sharding import PartitionSpec as P

MESH = pl.DeviceIdType.MESH
PRECISE = lax.Precision.HIGHEST
EPSILON = 1e-05
F32 = jnp.float32
BF16 = jnp.bfloat16
LANES = 128
HEADS_DEV = 10
WIDTH = 64
FEATS = HEADS_DEV * WIDTH
STATE = 128
CHUNK = 128
CHUNKS = 8
OUTS = 2560
LIFT = 9
GROUPS = ((0, 384), (384, 640))
TILE = OUTS // 4

NT = (((1,), (1,)), ((), ()))
TN = (((0,), (0,)), ((), ()))
NN = (((1,), (0,)), ((), ()))


def iota(shape, axis):
    return lax.broadcasted_iota(jnp.int32, shape, axis)


def dot(a, b, dims=NN):
    return lax.dot_general(a, b, dims, preferred_element_type=F32)


def exact(a, b, dims=NN):
    return lax.dot_general(a, b, dims, precision=PRECISE, preferred_element_type=F32)


def split(value, axis=1):
    high = value.astype(BF16)
    low = (value - high.astype(F32)).astype(BF16)
    return jnp.concatenate([high, low], axis=axis)


def split3(value):
    high = value.astype(BF16)
    rest = value - high.astype(F32)
    middle = rest.astype(BF16)
    return high, middle, (rest - middle.astype(F32)).astype(BF16)


def kernel(
    values,
    state_in,
    state_out,
    log_decay,
    level_class,
    level_table,
    skip_gain,
    norm_gain,
    weight,
    result,
    rows,
    entering,
    leaving,
    decay,
    classes,
    table,
    skip,
    gain,
    all_weight,
    expander,
    within,
    stretch,
    factors,
    mixers,
    readers,
    totals,
    row_factors,
    mix_factors,
    pair_state,
    quad_state,
    half_state,
    output,
    ring_x,
    ring_z,
    buckets,
    normed_send,
    normed_all,
    own_sum,
    rounded,
    held,
    partial_send,
    relay_recv,
    partial_recv,
    local_sem,
    a_send,
    a_recv,
    w1_send,
    w1_recv,
    w2_send,
    w2_recv,
    wf_send,
    wf_recv,
    t_send,
    t_recv,
    x_send,
    x_recv,
    z_send,
    z_recv,
    n_send,
    n_recv,
    r_send,
    r_recv,
    p_send,
    p_recv,
):
    ctx = lax.axis_index("ctx")
    head = lax.axis_index("head")
    x = lax.rem(ctx, 4)
    z = ctx // 4
    y = head // 2
    core = lax.rem(head, 2)
    partner = y * 2 + (1 - core)

    def copy(source, target, send, recv, device):
        return pltpu.make_async_remote_copy(
            src_ref=source,
            dst_ref=target,
            send_sem=send,
            recv_sem=recv,
            device_id=device,
            device_id_type=MESH,
        )

    barrier = pltpu.get_barrier_semaphore()
    for step in range(1, 8):
        pl.semaphore_signal(
            barrier,
            inc=1,
            device_id=(ctx, lax.rem(head + step, 8)),
            device_id_type=MESH,
        )
    def near_x(step):
        return z * 4 + lax.rem(x + step, 4)

    def near_z(step):
        return lax.rem(z + step, 4) * 4 + x

    for step in range(1, 4):
        for device in (near_x(step), near_z(step)):
            pl.semaphore_signal(
                barrier, inc=1, device_id=(device, head), device_id_type=MESH
            )

    loads = [
        pltpu.make_async_copy(source, target, local_sem.at[number])
        for number, (source, target) in enumerate(
            [
                (log_decay, decay),
                (level_class, classes),
                (level_table, table),
                (state_in, entering),
                (state_out, leaving),
                (skip_gain, skip),
                (norm_gain, gain),
            ]
        )
    ]
    for load in loads:
        load.start()
    own_lanes = pl.ds(pl.multiple_of(core * FEATS, LANES), FEATS)
    other_lanes = pl.ds(pl.multiple_of((1 - core) * FEATS, LANES), FEATS)
    my_rows = pl.ds(pl.multiple_of(core * CHUNK, CHUNK), CHUNK)
    for group, (low, high) in enumerate(GROUPS):
        pltpu.make_async_copy(
            values.at[:, pl.ds(pl.multiple_of(head * FEATS + low, LANES), high - low)],
            rows.at[y, my_rows, low:high],
            a_recv.at[group, 0],
        ).start()
    own_weight = pltpu.make_async_copy(
        weight, all_weight.at[z, x, :, :, own_lanes], local_sem.at[7]
    )
    own_weight.start()

    pl.semaphore_wait(barrier, 13)

    value_copies = []
    for group, (low, high) in enumerate(GROUPS):
        for number in (6, 7, 2, 3, 4, 5, 1):
            target = lax.rem(y + (0, 1, 3, 2)[number // 2], 4) * 2 + lax.rem(
                core + number % 2, 2
            )
            value_copies.append(
                copy(
                    values.at[
                        :, pl.ds(pl.multiple_of(target * FEATS + low, LANES), high - low)
                    ],
                    rows.at[y, my_rows, low:high],
                    a_send.at[group, number],
                    a_recv.at[group, number],
                    (ctx, target),
                )
            )
            value_copies[-1].start()

    first_copies = []
    for number, step in enumerate((2, 1, 3)):
        first_copies.append(
            copy(
                weight.at[0],
                all_weight.at[z, x, 0, :, own_lanes],
                w1_send.at[number],
                w1_recv.at[number],
                (near_x(step), head),
            )
        )
        first_copies.append(
            copy(
                weight.at[1],
                all_weight.at[z, x, 1, :, own_lanes],
                w1_send.at[3 + number],
                w1_recv.at[3 + number],
                (near_z(step), head),
            )
        )
    for item in first_copies:
        item.start()

    for load in loads:
        load.wait()
    spread = (
        (iota((HEADS_DEV, LANES), 1) % HEADS_DEV == iota((HEADS_DEV, LANES), 0))
        & (iota((HEADS_DEV, LANES), 1) < 100)
    ).astype(F32)
    lane_level = iota((CHUNK, LANES), 1) // HEADS_DEV
    causal = (iota((CHUNK, CHUNK), 0) >= iota((CHUNK, CHUNK), 1)) & (
        iota((CHUNK, CHUNK), 0) // 64 == iota((CHUNK, CHUNK), 1) // 64
    )
    causal_bf16 = causal.astype(F32).astype(BF16)
    causal_wide = jnp.concatenate([causal_bf16] * 3, axis=1)
    spread_bf16 = spread.astype(BF16)
    within[...] = sum(dot(part, spread_bf16, TN) for part in split3(decay[...]))
    first_half = iota((CHUNK, CHUNK), 1) < 64

    @pl.loop(0, CHUNKS)
    def _(j):
        tokens = pl.ds(pl.multiple_of(j * CHUNK, CHUNK), CHUNK)
        part = dot(causal_wide, jnp.concatenate(split3(within[tokens, :]), axis=0))
        within[tokens, :] = part
        stretch[pl.ds(j * 2, 1), :] = part[63:64, :]
        stretch[pl.ds(j * 2 + 1, 1), :] = part[127:128, :]

    sums = stretch[...]
    total_row = jnp.sum(sums, axis=0, keepdims=True)
    totals[z, x] = jnp.broadcast_to(total_row, (8, LANES))
    total_copies = []

    def share_totals(part, first, device):
        for step in range(1, 4):
            item = copy(
                part,
                part,
                t_send.at[first + step],
                t_recv.at[first + step],
                (device(step), head),
            )
            item.start()
            total_copies.append(item)

    def hear_totals(part, first):
        for step in range(1, 4):
            piece = part(step)
            copy(
                piece,
                piece,
                t_send.at[first + step],
                t_recv.at[first + step],
                (near_x(1), head),
            ).wait_recv()

    share_totals(totals.at[z, x], 0, near_x)

    expander[...] = (
        (iota((256, FEATS), 0) % LANES == iota((256, FEATS), 1) // WIDTH)
        .astype(F32)
        .astype(BF16)
    )

    late = iota((16, 16), 0)
    early = iota((16, 16), 1)
    small_level = iota((16, LANES), 1) // HEADS_DEV
    prefix = jnp.zeros((16, LANES), F32)
    for size, low, high in ((2, 2, 3), (4, 3, 4), (8, 4, 5), (16, 5, 9)):
        before = ((late // size == early // size) & (early < late)).astype(F32)
        prefix = jnp.where(
            (small_level >= low) & (small_level < high), exact(before, sums), prefix
        )
    stretch[...] = prefix

    block = iota((32, 16), 0)
    piece = iota((32, 16), 1)
    pick = (block < 16) & (piece == block)
    pick = pick | (
        (block >= 16) & (block < 20) & (piece // 2 == (block - 16) * 2 + 1)
    )
    pick = pick | (
        (block >= 20) & (block < 22) & (piece // 4 == (block - 20) * 2 + 1)
    )
    pick = pick | ((block == 22) & (piece >= 8))
    row_factors[...] = dot(
        split(jnp.exp(exact(pick.astype(F32), sums))), expander[...]
    )

    table_rows = jnp.zeros((32, LANES), F32)
    for level in range(9):
        table_rows = table_rows + exact(
            table[level],
            jnp.where(iota((HEADS_DEV, LANES), 1) // HEADS_DEV == level, spread, 0.0),
            TN,
        )
    table_wide = jnp.concatenate(split3(table_rows), axis=0)
    class_rows = iota((32, CHUNK), 0)
    lift_lane = (lane_level == LIFT).astype(F32)
    second_row = iota((CHUNK, LANES), 0) // 64

    @pl.loop(0, CHUNKS)
    def _(j):
        tokens = pl.ds(pl.multiple_of(j * CHUNK, CHUNK), CHUNK)
        onehot = (class_rows == classes[pl.ds(j, 1), :]).astype(F32).astype(BF16)
        weights = dot(jnp.concatenate([onehot] * 3, axis=0), table_wide, TN) + lift_lane
        part = within[tokens, :]
        start = jnp.where(
            second_row == 0, stretch[pl.ds(j * 2, 1), :], stretch[pl.ds(j * 2 + 1, 1), :]
        )
        exponent = jnp.where(lane_level == LIFT, -part, part + start)
        bit = jnp.where(
            lane_level == 1,
            second_row,
            jnp.where(
                lane_level == 2,
                lax.rem(j, 2),
                jnp.where(
                    lane_level == 3,
                    lax.rem(j // 2, 2),
                    jnp.where(lane_level == 4, j // 4, 1),
                ),
            ),
        )
        every = jnp.where(bit == 1, jnp.exp(exponent) * weights, 0.0)
        for level in range(10):
            turn = (LANES - level * HEADS_DEV) % LANES
            factors[level, tokens, :] = split(pltpu.roll(every, turn, 1) if turn else every)
        incoming = entering[tokens, :]
        reader = leaving[tokens, :]
        readers[tokens, :] = jnp.concatenate([reader, reader], axis=1)
        scores = jnp.where(causal, dot(reader, incoming, NT), 0.0)
        score_high = scores.astype(BF16)
        score_low = (scores - score_high.astype(F32)).astype(BF16)
        turned = incoming.astype(F32).T
        lower = jnp.where(first_half, turned, 0.0).astype(BF16)
        upper = jnp.where(first_half, 0.0, turned).astype(BF16)
        half = jnp.concatenate([score_high, score_low, lower, upper], axis=0)
        mixers[j] = jnp.concatenate([half, half], axis=1)

    skip_row = dot(split(exact(skip[...], spread)), expander[...])

    hear_totals(lambda step: totals.at[z, lax.rem(x + 4 - step, 4)], 0)
    share_totals(totals.at[z], 4, near_z)

    own_weight.wait()
    for item in first_copies:
        item.wait_recv()
    above_z = lax.rem(z + 1, 4)
    below_z = lax.rem(z + 3, 4)
    far_z = lax.rem(z + 2, 4)
    above_x = lax.rem(x + 1, 4)
    below_x = lax.rem(x + 3, 4)
    far_x = lax.rem(x + 2, 4)
    slabs = [
        lambda lanes: all_weight.at[z, :, 0, :, lanes],
        lambda lanes: all_weight.at[:, x, 1, :, lanes],
        lambda lanes: all_weight.at[below_z, :, 0, :, lanes],
        lambda lanes: all_weight.at[above_z, :, 0, :, lanes],
        lambda lanes: all_weight.at[:, below_x, 1, :, lanes],
        lambda lanes: all_weight.at[:, above_x, 1, :, lanes],
        lambda lanes: all_weight.at[far_z, 0:2, 0, :, lanes],
        lambda lanes: all_weight.at[far_z, 2:4, 0, :, lanes],
        lambda lanes: all_weight.at[0:2, far_x, 1, :, lanes],
        lambda lanes: all_weight.at[2:4, far_x, 1, :, lanes],
    ]
    second_copies = []
    forward_copies = []

    def pass_on(part, number, device):
        item = copy(part, part, w2_send.at[number], w2_recv.at[number], (device, head))
        item.start()
        second_copies.append(item)

    def arrived(number):
        part = slabs[number + 2](own_lanes)
        copy(
            part, part, w2_send.at[number], w2_recv.at[number], (near_z(1), head)
        ).wait_recv()

    def forward(number):
        part = slabs[number](own_lanes)
        item = copy(part, part, wf_send.at[number], wf_recv.at[number], (ctx, partner))
        item.start()
        forward_copies.append(item)

    pass_on(slabs[0](own_lanes), 0, near_z(1))
    pass_on(slabs[0](own_lanes), 1, near_z(3))
    pass_on(slabs[1](own_lanes), 2, near_x(1))
    pass_on(slabs[1](own_lanes), 3, near_x(3))
    forward(0)
    forward(1)

    def pair_work(pair, low, high):
        inputs = rows[pair, :, low:high].astype(F32)
        tokens = pl.ds(pl.multiple_of(pair * 256, 256), 256)
        expanded = dot(
            jnp.concatenate(
                [factors[LIFT, tokens, :], factors[0, tokens, :], factors[1, tokens, :]],
                axis=0,
            ),
            expander[:, low:high],
        )
        lifted = expanded[:256] * inputs
        states = []
        for half in range(2):
            start = half * CHUNK
            part = slice(start, start + CHUNK)
            j = pair * 2 + half
            product = dot(mixers[j], split(lifted[part], 0))
            lower_state = row_factors[pl.ds(j * 2, 1), :][:, low:high] * product[256:384]
            states.append(
                row_factors[pl.ds(j * 2 + 1, 1), :][:, low:high]
                * (lower_state + product[384:512])
            )
            gained = dot(
                readers[pl.ds(pl.multiple_of(j * CHUNK, CHUNK), CHUNK), :],
                split(lower_state, 0),
            )
            output[pair, part, low:high] = (
                expanded[256 + start : 384 + start] * (product[:128] + product[128:256])
                + expanded[512 + start : 640 + start] * gained
                + skip_row[:, low:high] * inputs[part]
            )
        pair_state[pair, :, low:high] = states[0]
        quad_state[pair, :, low:high] = (
            row_factors[pl.ds(16 + pair, 1), :][:, low:high] * states[0] + states[1]
        )

    x_copies = []
    for group, (low, high) in enumerate(GROUPS):

        @pl.loop(0, 4)
        def _(order):
            step = order + (order // 2) * (1 - 2 * lax.rem(order, 2))
            pair = lax.rem(y + 4 - step, 4)
            for half in range(2):
                place = rows.at[pair, half * CHUNK : (half + 1) * CHUNK, low:high]
                pltpu.make_async_copy(
                    place, place, a_recv.at[group, order * 2 + half]
                ).wait()
            pair_work(pair, low, high)

        for half in range(2):
            half_state[half, :, low:high] = (
                row_factors[20 + half : 21 + half, low:high]
                * quad_state[2 * half, :, low:high]
                + quad_state[2 * half + 1, :, low:high]
            )
        ring_x[x, :, low:high] = (
            row_factors[22:23, low:high] * half_state[0, :, low:high]
            + half_state[1, :, low:high]
        ).astype(BF16)
        for number, step in enumerate((2, 1, 3)):
            x_copies.append(
                copy(
                    ring_x.at[x, :, low:high],
                    ring_x.at[x, :, low:high],
                    x_send.at[group, number],
                    x_recv.at[group, number],
                    (near_x(step), head),
                )
            )
            x_copies[-1].start()
        if group == 0:
            hear_totals(lambda step: totals.at[lax.rem(z + 4 - step, 4)], 4)
            every_total = jnp.concatenate(
                [totals[d // 4, d % 4][0:1, :] for d in range(16)], axis=0
            )
            row = iota((32, 16), 0)
            shard = iota((32, 16), 1)
            kind = row // 4
            slot = row % 4
            shard_x = shard % 4
            shard_z = shard // 4
            same_z = shard_z == z
            counted = (kind == 1) & same_z & (shard_x > slot) & (shard_x < x)
            counted = counted | ((kind == 2) & same_z & (shard_x > slot))
            counted = counted | ((kind >= 3) & (kind < 5) & same_z & (shard_x < x))
            counted = counted | ((kind == 4) & (shard_z > slot) & (shard_z < z))
            row = iota((32, LANES), 0)
            kind = row // 4
            slot = row % 4
            used = (kind == 0) & (slot == x - 1) & (lax.rem(x, 2) == 1)
            used = used | ((kind == 1) & (x >= 2) & (slot < 2))
            used = used | (kind == 2)
            used = used | ((kind == 3) & (slot == z - 1) & (lax.rem(z, 2) == 1))
            used = used | ((kind == 4) & (z >= 2) & (slot < 2))
            mix = jnp.where(used, jnp.exp(exact(counted.astype(F32), every_total)), 0.0)
            mix_factors[...] = dot(split(mix), expander[...])

    def mixed(ring, start, low, high):
        total = jnp.zeros((STATE, high - low), F32)
        for source in range(4):
            total = total + mix_factors[
                start + source : start + source + 1, low:high
            ] * ring[source, :, low:high].astype(F32)
        return total

    def hear(ring, recv, group, low, high, position, device):
        for number, step in enumerate((2, 1, 3)):
            origin = lax.rem(position + 4 - step, 4)
            copy(
                ring.at[origin, :, low:high],
                ring.at[origin, :, low:high],
                x_send.at[group, number],
                recv.at[group, number],
                (device(origin), head),
            ).wait_recv()

    def read_local(step):
        def rows_of(start, count):
            return pl.ds(pl.multiple_of(start, CHUNK), count)

        first = rows_of(step * 512 + 128, 128)
        second = rows_of(step * 512 + 384, 128)
        third = rows_of(step * 512 + 256, 256)
        fourth = rows_of(512 + step * 256, 256)
        expanded = dot(
            jnp.concatenate(
                [
                    factors[2, first, :],
                    factors[2, second, :],
                    factors[3, third, :],
                    factors[4, fourth, :],
                ],
                axis=0,
            ),
            expander[...],
        )
        upper = slice(CHUNK, 2 * CHUNK)
        output[step * 2, upper, :] += expanded[:128] * dot(
            readers[first, :], split(pair_state[step * 2], 0)
        )
        output[step * 2 + 1, upper, :] += expanded[128:256] * dot(
            readers[second, :], split(pair_state[step * 2 + 1], 0)
        )
        output[step * 2 + 1] += expanded[256:512] * dot(
            readers[third, :], split(quad_state[step * 2], 0)
        )
        output[2 + step] += expanded[512:] * dot(
            readers[fourth, :], split(half_state[0], 0)
        )

    arrived(0)
    arrived(1)
    pass_on(all_weight.at[below_z, 0:2, 0, :, own_lanes], 4, near_z(1))
    pass_on(all_weight.at[above_z, 2:4, 0, :, own_lanes], 5, near_z(3))
    forward(2)
    forward(3)
    pl.loop(0, 2)(read_local)

    z_copies = []
    for group, (low, high) in enumerate(GROUPS):
        hear(ring_x, x_recv, group, low, high, x, lambda origin: z * 4 + origin)
        ring_z[z, :, low:high] = mixed(ring_x, 8, low, high).astype(BF16)
        for number, step in enumerate((2, 1, 3)):
            z_copies.append(
                copy(
                    ring_z.at[z, :, low:high],
                    ring_z.at[z, :, low:high],
                    z_send.at[group, number],
                    z_recv.at[group, number],
                    (near_z(step), head),
                )
            )
            z_copies[-1].start()
        buckets[0, :, low:high] = split(mixed(ring_x, 0, low, high), 0)
        buckets[1, :, low:high] = split(mixed(ring_x, 4, low, high), 0)

    arrived(2)
    arrived(3)
    pass_on(all_weight.at[0:2, below_x, 1, :, own_lanes], 6, near_x(1))
    pass_on(all_weight.at[2:4, above_x, 1, :, own_lanes], 7, near_x(3))
    forward(4)
    forward(5)

    def read_levels(start, count, low):
        tokens = pl.ds(pl.multiple_of(start, CHUNK), count)
        reader = readers[tokens, :]
        expanded = dot(
            jnp.concatenate([factors[low, tokens, :], factors[low + 1, tokens, :]], axis=0),
            expander[...],
        )
        return expanded[:count] * dot(reader, buckets[0]) + expanded[count:] * dot(
            reader, buckets[1]
        )

    @pl.loop(0, 4)
    def _(pair):
        output[pair] = output[pair] + read_levels(pair * 256, 256, 5)

    for number in (4, 5, 6, 7):
        arrived(number)
        forward(number + 2)

    for group, (low, high) in enumerate(GROUPS):
        hear(ring_z, z_recv, group, low, high, z, lambda origin: origin * 4 + x)
        buckets[0, :, low:high] = split(mixed(ring_z, 12, low, high), 0)
        buckets[1, :, low:high] = split(mixed(ring_z, 16, low, high), 0)

    same_head = (
        iota((256, LANES), 0) % LANES // WIDTH == iota((256, LANES), 1) // WIDTH
    ).astype(F32).astype(BF16)

    gain_row = gain[...].reshape(1, FEATS)

    def finish(pair, side):
        here = pl.ds(pl.multiple_of(side * CHUNK, CHUNK), CHUNK)
        total = output[pair, here, :] + read_levels(pair * 256 + side * CHUNK, CHUNK, 7)
        pieces = []
        for group in range(FEATS // LANES):
            part = total[:, group * LANES : (group + 1) * LANES]
            mean_square = dot(split(part * part), same_head) * (1.0 / WIDTH)
            scaled = part * lax.rsqrt(mean_square + EPSILON)
            pieces.append(scaled * gain_row[:, group * LANES : (group + 1) * LANES])
        return jnp.concatenate(pieces, axis=1).astype(BF16)

    def place_chip(place):
        return lax.rem(y + (2, 1, 3, 0)[place], 4)

    normed_copies = []

    def hand_over(place):
        normed_send[place] = finish(place_chip(place), 1 - core)
        normed_copies.append(
            copy(
                normed_send.at[place],
                normed_all.at[place, :, own_lanes],
                n_send.at[place],
                n_recv.at[place],
                (ctx, partner),
            )
        )
        normed_copies[-1].start()

    def keep(place):
        normed_all[place, :, own_lanes] = finish(place_chip(place), core)

    hand_over(0)
    keep(0)
    hand_over(1)
    for number, slab in enumerate(slabs):
        copy(
            slab(other_lanes),
            slab(other_lanes),
            wf_send.at[number],
            wf_recv.at[number],
            (ctx, partner),
        ).wait_recv()

    up = (ctx, lax.rem(y + 1, 4) * 2 + core)
    down = (ctx, lax.rem(y + 3, 4) * 2 + core)
    partial_copies = []

    def product(first_place, last_place, quarter):
        count = last_place - first_place
        return dot(
            normed_all[first_place:last_place].reshape(count * CHUNK, 2 * FEATS),
            all_weight[quarter].reshape(TILE, 2 * FEATS),
            NT,
        )

    def send(value, place, quarter, target, send_sems, recv_sems, device):
        partial_send[place, quarter] = value.astype(BF16)
        item = copy(
            partial_send.at[place, quarter], target, send_sems, recv_sems, device
        )
        item.start()
        partial_copies.append(item)

    normed_copies[0].wait_recv()
    for quarter in (0, 2, 1, 3):
        send(
            product(0, 1, quarter),
            0,
            quarter,
            relay_recv.at[quarter],
            r_send.at[quarter],
            r_recv.at[quarter],
            up if quarter < 2 else down,
        )
    keep(1)
    hand_over(2)
    keep(2)
    normed_copies[1].wait_recv()
    normed_copies[2].wait_recv()

    def send_near(value, place, quarter):
        send(
            value,
            place,
            quarter,
            partial_recv.at[place - 1, quarter],
            p_send.at[place - 1, quarter],
            p_recv.at[place - 1, quarter],
            up if place == 1 else down,
        )

    for quarter in (2, 0, 3, 1):
        both = product(1, 3, quarter)
        if quarter < 2:
            held[quarter] = both[:CHUNK]
            send_near(both[CHUNK:], 2, quarter)
        else:
            send_near(both[:CHUNK], 1, quarter)
            held[quarter] = both[CHUNK:]
    hand_over(3)
    keep(3)
    for quarter in (0, 2, 1, 3):
        partial_copies[(0, 2, 1, 3).index(quarter)].wait_recv()
        send_near(
            held[quarter] + relay_recv[quarter].astype(F32),
            1 if quarter < 2 else 2,
            quarter,
        )
    normed_copies[3].wait_recv()
    for quarter in range(4):
        own_sum[:, quarter * TILE : (quarter + 1) * TILE] = product(3, 4, quarter)
    result_copies = []
    for quarter in (2, 0, 3, 1):
        for place in range(2):
            copy(
                partial_recv.at[place, quarter],
                partial_recv.at[place, quarter],
                p_send.at[place, quarter],
                p_recv.at[place, quarter],
                up,
            ).wait_recv()
        columns = slice(quarter * TILE, (quarter + 1) * TILE)
        rounded[:, columns] = (
            own_sum[:, columns]
            + partial_recv[0, quarter].astype(F32)
            + partial_recv[1, quarter].astype(F32)
        ).astype(BF16)
        result_copies.append(
            pltpu.make_async_copy(
                rounded.at[:, columns], result.at[:, columns], local_sem.at[quarter]
            )
        )
        result_copies[-1].start()
    for item in result_copies:
        item.wait()

    for item in (
        value_copies
        + first_copies
        + total_copies
        + second_copies
        + forward_copies
        + x_copies
        + z_copies
        + normed_copies
        + partial_copies
    ):
        item.wait_send()


def on_device(
    values,
    state_in,
    state_out,
    log_decay,
    level_class,
    level_table,
    skip_gain,
    norm_gain,
    out_weight,
):
    columns = out_weight.shape[1]
    weight = out_weight.T.reshape(2, columns // 2, FEATS)
    anywhere = pl.BlockSpec(memory_space=pl.ANY)
    dma = pltpu.SemaphoreType.DMA
    groups = len(GROUPS)
    return pl.pallas_call(
        kernel,
        out_shape=jax.ShapeDtypeStruct((CHUNK, OUTS), BF16),
        in_specs=[anywhere] * 9,
        out_specs=anywhere,
        scratch_shapes=[
            pltpu.VMEM((4, 2 * CHUNK, FEATS), BF16),
            pltpu.VMEM((CHUNKS * CHUNK, STATE), BF16),
            pltpu.VMEM((CHUNKS * CHUNK, STATE), BF16),
            pltpu.VMEM((HEADS_DEV, CHUNKS * CHUNK), F32),
            pltpu.VMEM((CHUNKS, CHUNK), jnp.int32),
            pltpu.VMEM((9, HEADS_DEV, 32), F32),
            pltpu.VMEM((1, HEADS_DEV), F32),
            pltpu.VMEM((FEATS,), F32),
            pltpu.VMEM((4, 4, 2, 80, 2 * FEATS), BF16),
            pltpu.VMEM((256, FEATS), BF16),
            pltpu.VMEM((CHUNKS * CHUNK, LANES), F32),
            pltpu.VMEM((16, LANES), F32),
            pltpu.VMEM((10, CHUNKS * CHUNK, 2 * LANES), BF16),
            pltpu.VMEM((CHUNKS, 4 * CHUNK, 2 * STATE), BF16),
            pltpu.VMEM((CHUNKS * CHUNK, 2 * STATE), BF16),
            pltpu.VMEM((4, 4, 8, LANES), F32),
            pltpu.VMEM((32, FEATS), F32),
            pltpu.VMEM((32, FEATS), F32),
            pltpu.VMEM((4, STATE, FEATS), F32),
            pltpu.VMEM((4, STATE, FEATS), F32),
            pltpu.VMEM((2, STATE, FEATS), F32),
            pltpu.VMEM((4, 2 * CHUNK, FEATS), F32),
            pltpu.VMEM((4, STATE, FEATS), BF16),
            pltpu.VMEM((4, STATE, FEATS), BF16),
            pltpu.VMEM((2, 2 * STATE, FEATS), BF16),
            pltpu.VMEM((4, CHUNK, FEATS), BF16),
            pltpu.VMEM((4, CHUNK, 2 * FEATS), BF16),
            pltpu.VMEM((CHUNK, OUTS), F32),
            pltpu.VMEM((CHUNK, OUTS), BF16),
            pltpu.VMEM((4, CHUNK, TILE), F32),
            pltpu.VMEM((3, 4, CHUNK, TILE), BF16),
            pltpu.VMEM((4, CHUNK, TILE), BF16),
            pltpu.VMEM((2, 4, CHUNK, TILE), BF16),
            dma((8,)),
            dma((groups, 8)),
            dma((groups, 8)),
            dma((6,)),
            dma((6,)),
            dma((8,)),
            dma((8,)),
            dma((10,)),
            dma((10,)),
            dma((8,)),
            dma((8,)),
            dma((groups, 3)),
            dma((groups, 3)),
            dma((groups, 3)),
            dma((groups, 3)),
            dma((4,)),
            dma((4,)),
            dma((4,)),
            dma((4,)),
            dma((2, 4)),
            dma((2, 4)),
        ],
        compiler_params=pltpu.CompilerParams(
            collective_id=0,
            has_side_effects=True,
            vmem_limit_bytes=60 * 1024 * 1024,
        ),
        name="layer",
    )(
        values,
        state_in,
        state_out,
        log_decay.T,
        level_class.reshape(CHUNKS, CHUNK),
        level_table.transpose(1, 2, 0),
        skip_gain.reshape(1, -1),
        norm_gain,
        weight,
    )


def solution(mesh):
    return jax.shard_map(
        on_device,
        mesh=mesh,
        in_specs=(
            P(("ctx", "head"), None),
            P("ctx", None),
            P("ctx", None),
            P("ctx", "head"),
            P("ctx"),
            P(None, None, "head"),
            P("head"),
            P("head"),
            P("head", "ctx"),
        ),
        out_specs=P(("ctx", "head"), None),
        check_vma=False,
    )
```

```python
import jax
import jax.numpy as jnp
from jax import lax
from jax.experimental import pallas as pl
from jax.experimental.pallas import tpu as pltpu
from jax.sharding import PartitionSpec as P

MESH = pl.DeviceIdType.MESH
PRECISE = lax.Precision.HIGHEST
EPSILON = 1e-05
F32 = jnp.float32
BF16 = jnp.bfloat16
LANES = 128
HEADS_DEV = 10
WIDTH = 64
FEATS = HEADS_DEV * WIDTH
STATE = 128
CHUNK = 128
CHUNKS = 8
OUTS = 2560
LIFT = 9
GROUPS = ((0, 384), (384, 640))
TILE = OUTS // 4

NT = (((1,), (1,)), ((), ()))
TN = (((0,), (0,)), ((), ()))
NN = (((1,), (0,)), ((), ()))


def iota(shape, axis):
    return lax.broadcasted_iota(jnp.int32, shape, axis)


def dot(a, b, dims=NN):
    return lax.dot_general(a, b, dims, preferred_element_type=F32)


def exact(a, b, dims=NN):
    return lax.dot_general(a, b, dims, precision=PRECISE, preferred_element_type=F32)


def split(value, axis=1):
    high = value.astype(BF16)
    low = (value - high.astype(F32)).astype(BF16)
    return jnp.concatenate([high, low], axis=axis)


def split3(value):
    high = value.astype(BF16)
    rest = value - high.astype(F32)
    middle = rest.astype(BF16)
    return high, middle, (rest - middle.astype(F32)).astype(BF16)


def kernel(
    values,
    state_in,
    state_out,
    log_decay,
    level_class,
    level_table,
    skip_gain,
    norm_gain,
    weight,
    result,
    rows,
    entering,
    leaving,
    decay,
    classes,
    table,
    skip,
    gain,
    all_weight,
    expander,
    within,
    stretch,
    factors,
    mixers,
    readers,
    totals,
    row_factors,
    mix_factors,
    pair_state,
    quad_state,
    half_state,
    output,
    ring_x,
    ring_z,
    buckets,
    normed_send,
    normed_all,
    own_sum,
    held,
    partial_send,
    relay_recv,
    partial_recv,
    local_sem,
    a_send,
    a_recv,
    w1_send,
    w1_recv,
    w2_send,
    w2_recv,
    wf_send,
    wf_recv,
    t_send,
    t_recv,
    x_send,
    x_recv,
    z_send,
    z_recv,
    n_send,
    n_recv,
    r_send,
    r_recv,
    p_send,
    p_recv,
):
    ctx = lax.axis_index("ctx")
    head = lax.axis_index("head")
    x = lax.rem(ctx, 4)
    z = ctx // 4
    y = head // 2
    core = lax.rem(head, 2)
    partner = y * 2 + (1 - core)

    def copy(source, target, send, recv, device):
        return pltpu.make_async_remote_copy(
            src_ref=source,
            dst_ref=target,
            send_sem=send,
            recv_sem=recv,
            device_id=device,
            device_id_type=MESH,
        )

    barrier = pltpu.get_barrier_semaphore()
    for step in range(1, 8):
        pl.semaphore_signal(
            barrier,
            inc=1,
            device_id=(ctx, lax.rem(head + step, 8)),
            device_id_type=MESH,
        )
    def near_x(step):
        return z * 4 + lax.rem(x + step, 4)

    def near_z(step):
        return lax.rem(z + step, 4) * 4 + x

    for step in range(1, 4):
        for device in (near_x(step), near_z(step)):
            pl.semaphore_signal(
                barrier, inc=1, device_id=(device, head), device_id_type=MESH
            )

    loads = [
        pltpu.make_async_copy(source, target, local_sem.at[number])
        for number, (source, target) in enumerate(
            [
                (log_decay, decay),
                (level_class, classes),
                (level_table, table),
                (state_in, entering),
                (state_out, leaving),
                (skip_gain, skip),
                (norm_gain, gain),
            ]
        )
    ]
    for load in loads:
        load.start()
    own_lanes = pl.ds(pl.multiple_of(core * FEATS, LANES), FEATS)
    other_lanes = pl.ds(pl.multiple_of((1 - core) * FEATS, LANES), FEATS)
    my_rows = pl.ds(pl.multiple_of(core * CHUNK, CHUNK), CHUNK)
    for group, (low, high) in enumerate(GROUPS):
        pltpu.make_async_copy(
            values.at[:, pl.ds(pl.multiple_of(head * FEATS + low, LANES), high - low)],
            rows.at[y, my_rows, low:high],
            a_recv.at[group, 0],
        ).start()
    own_weight = pltpu.make_async_copy(
        weight, all_weight.at[z, x, :, :, own_lanes], local_sem.at[7]
    )
    own_weight.start()

    pl.semaphore_wait(barrier, 13)

    value_copies = []
    for group, (low, high) in enumerate(GROUPS):
        for number in (6, 7, 2, 3, 4, 5, 1):
            target = lax.rem(y + (0, 1, 3, 2)[number // 2], 4) * 2 + lax.rem(
                core + number % 2, 2
            )
            value_copies.append(
                copy(
                    values.at[
                        :, pl.ds(pl.multiple_of(target * FEATS + low, LANES), high - low)
                    ],
                    rows.at[y, my_rows, low:high],
                    a_send.at[group, number],
                    a_recv.at[group, number],
                    (ctx, target),
                )
            )
            value_copies[-1].start()

    first_copies = []
    for number, step in enumerate((2, 1, 3)):
        first_copies.append(
            copy(
                weight.at[0],
                all_weight.at[z, x, 0, :, own_lanes],
                w1_send.at[number],
                w1_recv.at[number],
                (near_x(step), head),
            )
        )
        first_copies.append(
            copy(
                weight.at[1],
                all_weight.at[z, x, 1, :, own_lanes],
                w1_send.at[3 + number],
                w1_recv.at[3 + number],
                (near_z(step), head),
            )
        )
    for item in first_copies:
        item.start()

    for load in loads:
        load.wait()
    spread = (
        (iota((HEADS_DEV, LANES), 1) % HEADS_DEV == iota((HEADS_DEV, LANES), 0))
        & (iota((HEADS_DEV, LANES), 1) < 100)
    ).astype(F32)
    lane_level = iota((CHUNK, LANES), 1) // HEADS_DEV
    causal = (iota((CHUNK, CHUNK), 0) >= iota((CHUNK, CHUNK), 1)) & (
        iota((CHUNK, CHUNK), 0) // 64 == iota((CHUNK, CHUNK), 1) // 64
    )
    causal_bf16 = causal.astype(F32).astype(BF16)
    causal_wide = jnp.concatenate([causal_bf16] * 3, axis=1)
    spread_bf16 = spread.astype(BF16)
    within[...] = sum(dot(part, spread_bf16, TN) for part in split3(decay[...]))
    first_half = iota((CHUNK, CHUNK), 1) < 64

    @pl.loop(0, CHUNKS)
    def _(j):
        tokens = pl.ds(pl.multiple_of(j * CHUNK, CHUNK), CHUNK)
        part = dot(causal_wide, jnp.concatenate(split3(within[tokens, :]), axis=0))
        within[tokens, :] = part
        stretch[pl.ds(j * 2, 1), :] = part[63:64, :]
        stretch[pl.ds(j * 2 + 1, 1), :] = part[127:128, :]

    sums = stretch[...]
    total_row = jnp.sum(sums, axis=0, keepdims=True)
    totals[z, x] = jnp.broadcast_to(total_row, (8, LANES))
    total_copies = []

    def share_totals(part, first, device):
        for step in range(1, 4):
            item = copy(
                part,
                part,
                t_send.at[first + step],
                t_recv.at[first + step],
                (device(step), head),
            )
            item.start()
            total_copies.append(item)

    def hear_totals(part, first):
        for step in range(1, 4):
            piece = part(step)
            copy(
                piece,
                piece,
                t_send.at[first + step],
                t_recv.at[first + step],
                (near_x(1), head),
            ).wait_recv()

    share_totals(totals.at[z, x], 0, near_x)

    expander[...] = (
        (iota((256, FEATS), 0) % LANES == iota((256, FEATS), 1) // WIDTH)
        .astype(F32)
        .astype(BF16)
    )

    late = iota((16, 16), 0)
    early = iota((16, 16), 1)
    small_level = iota((16, LANES), 1) // HEADS_DEV
    prefix = jnp.zeros((16, LANES), F32)
    for size, low, high in ((2, 2, 3), (4, 3, 4), (8, 4, 5), (16, 5, 9)):
        before = ((late // size == early // size) & (early < late)).astype(F32)
        prefix = jnp.where(
            (small_level >= low) & (small_level < high), exact(before, sums), prefix
        )
    stretch[...] = prefix

    block = iota((32, 16), 0)
    piece = iota((32, 16), 1)
    pick = (block < 16) & (piece == block)
    pick = pick | (
        (block >= 16) & (block < 20) & (piece // 2 == (block - 16) * 2 + 1)
    )
    pick = pick | (
        (block >= 20) & (block < 22) & (piece // 4 == (block - 20) * 2 + 1)
    )
    pick = pick | ((block == 22) & (piece >= 8))
    row_factors[...] = dot(
        split(jnp.exp(exact(pick.astype(F32), sums))), expander[...]
    )

    table_rows = jnp.zeros((32, LANES), F32)
    for level in range(9):
        table_rows = table_rows + exact(
            table[level],
            jnp.where(iota((HEADS_DEV, LANES), 1) // HEADS_DEV == level, spread, 0.0),
            TN,
        )
    table_wide = jnp.concatenate(split3(table_rows), axis=0)
    class_rows = iota((32, CHUNK), 0)
    lift_lane = (lane_level == LIFT).astype(F32)
    second_row = iota((CHUNK, LANES), 0) // 64

    @pl.loop(0, CHUNKS)
    def _(j):
        tokens = pl.ds(pl.multiple_of(j * CHUNK, CHUNK), CHUNK)
        onehot = (class_rows == classes[pl.ds(j, 1), :]).astype(F32).astype(BF16)
        weights = dot(jnp.concatenate([onehot] * 3, axis=0), table_wide, TN) + lift_lane
        part = within[tokens, :]
        start = jnp.where(
            second_row == 0, stretch[pl.ds(j * 2, 1), :], stretch[pl.ds(j * 2 + 1, 1), :]
        )
        exponent = jnp.where(lane_level == LIFT, -part, part + start)
        bit = jnp.where(
            lane_level == 1,
            second_row,
            jnp.where(
                lane_level == 2,
                lax.rem(j, 2),
                jnp.where(
                    lane_level == 3,
                    lax.rem(j // 2, 2),
                    jnp.where(lane_level == 4, j // 4, 1),
                ),
            ),
        )
        every = jnp.where(bit == 1, jnp.exp(exponent) * weights, 0.0)
        for level in range(10):
            turn = (LANES - level * HEADS_DEV) % LANES
            factors[level, tokens, :] = split(pltpu.roll(every, turn, 1) if turn else every)
        incoming = entering[tokens, :]
        reader = leaving[tokens, :]
        readers[tokens, :] = jnp.concatenate([reader, reader], axis=1)
        scores = jnp.where(causal, dot(reader, incoming, NT), 0.0)
        score_high = scores.astype(BF16)
        score_low = (scores - score_high.astype(F32)).astype(BF16)
        turned = incoming.astype(F32).T
        lower = jnp.where(first_half, turned, 0.0).astype(BF16)
        upper = jnp.where(first_half, 0.0, turned).astype(BF16)
        half = jnp.concatenate([score_high, score_low, lower, upper], axis=0)
        mixers[j] = jnp.concatenate([half, half], axis=1)

    skip_row = dot(split(exact(skip[...], spread)), expander[...])

    hear_totals(lambda step: totals.at[z, lax.rem(x + 4 - step, 4)], 0)
    share_totals(totals.at[z], 4, near_z)

    own_weight.wait()
    for item in first_copies:
        item.wait_recv()
    above_z = lax.rem(z + 1, 4)
    below_z = lax.rem(z + 3, 4)
    far_z = lax.rem(z + 2, 4)
    above_x = lax.rem(x + 1, 4)
    below_x = lax.rem(x + 3, 4)
    far_x = lax.rem(x + 2, 4)
    slabs = [
        lambda lanes: all_weight.at[z, :, 0, :, lanes],
        lambda lanes: all_weight.at[:, x, 1, :, lanes],
        lambda lanes: all_weight.at[below_z, :, 0, :, lanes],
        lambda lanes: all_weight.at[above_z, :, 0, :, lanes],
        lambda lanes: all_weight.at[:, below_x, 1, :, lanes],
        lambda lanes: all_weight.at[:, above_x, 1, :, lanes],
        lambda lanes: all_weight.at[far_z, 0:2, 0, :, lanes],
        lambda lanes: all_weight.at[far_z, 2:4, 0, :, lanes],
        lambda lanes: all_weight.at[0:2, far_x, 1, :, lanes],
        lambda lanes: all_weight.at[2:4, far_x, 1, :, lanes],
    ]
    second_copies = []
    forward_copies = []

    def pass_on(part, number, device):
        item = copy(part, part, w2_send.at[number], w2_recv.at[number], (device, head))
        item.start()
        second_copies.append(item)

    def arrived(number):
        part = slabs[number + 2](own_lanes)
        copy(
            part, part, w2_send.at[number], w2_recv.at[number], (near_z(1), head)
        ).wait_recv()

    def forward(number):
        part = slabs[number](own_lanes)
        item = copy(part, part, wf_send.at[number], wf_recv.at[number], (ctx, partner))
        item.start()
        forward_copies.append(item)

    pass_on(slabs[0](own_lanes), 0, near_z(1))
    pass_on(slabs[0](own_lanes), 1, near_z(3))
    pass_on(slabs[1](own_lanes), 2, near_x(1))
    pass_on(slabs[1](own_lanes), 3, near_x(3))
    forward(0)
    forward(1)

    def pair_work(pair, low, high):
        inputs = rows[pair, :, low:high].astype(F32)
        tokens = pl.ds(pl.multiple_of(pair * 256, 256), 256)
        expanded = dot(
            jnp.concatenate(
                [factors[LIFT, tokens, :], factors[0, tokens, :], factors[1, tokens, :]],
                axis=0,
            ),
            expander[:, low:high],
        )
        lifted = expanded[:256] * inputs
        states = []
        for half in range(2):
            start = half * CHUNK
            part = slice(start, start + CHUNK)
            j = pair * 2 + half
            product = dot(mixers[j], split(lifted[part], 0))
            lower_state = row_factors[pl.ds(j * 2, 1), :][:, low:high] * product[256:384]
            states.append(
                row_factors[pl.ds(j * 2 + 1, 1), :][:, low:high]
                * (lower_state + product[384:512])
            )
            gained = dot(
                readers[pl.ds(pl.multiple_of(j * CHUNK, CHUNK), CHUNK), :],
                split(lower_state, 0),
            )
            output[pair, part, low:high] = (
                expanded[256 + start : 384 + start] * (product[:128] + product[128:256])
                + expanded[512 + start : 640 + start] * gained
                + skip_row[:, low:high] * inputs[part]
            )
        pair_state[pair, :, low:high] = states[0]
        quad_state[pair, :, low:high] = (
            row_factors[pl.ds(16 + pair, 1), :][:, low:high] * states[0] + states[1]
        )

    x_copies = []
    for group, (low, high) in enumerate(GROUPS):

        @pl.loop(0, 4)
        def _(order):
            step = order + (order // 2) * (1 - 2 * lax.rem(order, 2))
            pair = lax.rem(y + 4 - step, 4)
            for half in range(2):
                place = rows.at[pair, half * CHUNK : (half + 1) * CHUNK, low:high]
                pltpu.make_async_copy(
                    place, place, a_recv.at[group, order * 2 + half]
                ).wait()
            pair_work(pair, low, high)

        for half in range(2):
            half_state[half, :, low:high] = (
                row_factors[20 + half : 21 + half, low:high]
                * quad_state[2 * half, :, low:high]
                + quad_state[2 * half + 1, :, low:high]
            )
        ring_x[x, :, low:high] = (
            row_factors[22:23, low:high] * half_state[0, :, low:high]
            + half_state[1, :, low:high]
        ).astype(BF16)
        for number, step in enumerate((2, 1, 3)):
            x_copies.append(
                copy(
                    ring_x.at[x, :, low:high],
                    ring_x.at[x, :, low:high],
                    x_send.at[group, number],
                    x_recv.at[group, number],
                    (near_x(step), head),
                )
            )
            x_copies[-1].start()
        if group == 0:
            hear_totals(lambda step: totals.at[lax.rem(z + 4 - step, 4)], 4)
            every_total = jnp.concatenate(
                [totals[d // 4, d % 4][0:1, :] for d in range(16)], axis=0
            )
            row = iota((32, 16), 0)
            shard = iota((32, 16), 1)
            kind = row // 4
            slot = row % 4
            shard_x = shard % 4
            shard_z = shard // 4
            same_z = shard_z == z
            counted = (kind == 1) & same_z & (shard_x > slot) & (shard_x < x)
            counted = counted | ((kind == 2) & same_z & (shard_x > slot))
            counted = counted | ((kind >= 3) & (kind < 5) & same_z & (shard_x < x))
            counted = counted | ((kind == 4) & (shard_z > slot) & (shard_z < z))
            row = iota((32, LANES), 0)
            kind = row // 4
            slot = row % 4
            used = (kind == 0) & (slot == x - 1) & (lax.rem(x, 2) == 1)
            used = used | ((kind == 1) & (x >= 2) & (slot < 2))
            used = used | (kind == 2)
            used = used | ((kind == 3) & (slot == z - 1) & (lax.rem(z, 2) == 1))
            used = used | ((kind == 4) & (z >= 2) & (slot < 2))
            mix = jnp.where(used, jnp.exp(exact(counted.astype(F32), every_total)), 0.0)
            mix_factors[...] = dot(split(mix), expander[...])

    def mixed(ring, start, low, high):
        total = jnp.zeros((STATE, high - low), F32)
        for source in range(4):
            total = total + mix_factors[
                start + source : start + source + 1, low:high
            ] * ring[source, :, low:high].astype(F32)
        return total

    def hear(ring, recv, group, low, high, position, device):
        for number, step in enumerate((2, 1, 3)):
            origin = lax.rem(position + 4 - step, 4)
            copy(
                ring.at[origin, :, low:high],
                ring.at[origin, :, low:high],
                x_send.at[group, number],
                recv.at[group, number],
                (device(origin), head),
            ).wait_recv()

    def read_local(step):
        def rows_of(start, count):
            return pl.ds(pl.multiple_of(start, CHUNK), count)

        first = rows_of(step * 512 + 128, 128)
        second = rows_of(step * 512 + 384, 128)
        third = rows_of(step * 512 + 256, 256)
        fourth = rows_of(512 + step * 256, 256)
        expanded = dot(
            jnp.concatenate(
                [
                    factors[2, first, :],
                    factors[2, second, :],
                    factors[3, third, :],
                    factors[4, fourth, :],
                ],
                axis=0,
            ),
            expander[...],
        )
        upper = slice(CHUNK, 2 * CHUNK)
        output[step * 2, upper, :] += expanded[:128] * dot(
            readers[first, :], split(pair_state[step * 2], 0)
        )
        output[step * 2 + 1, upper, :] += expanded[128:256] * dot(
            readers[second, :], split(pair_state[step * 2 + 1], 0)
        )
        output[step * 2 + 1] += expanded[256:512] * dot(
            readers[third, :], split(quad_state[step * 2], 0)
        )
        output[2 + step] += expanded[512:] * dot(
            readers[fourth, :], split(half_state[0], 0)
        )

    arrived(0)
    arrived(1)
    pass_on(all_weight.at[below_z, 0:2, 0, :, own_lanes], 4, near_z(1))
    pass_on(all_weight.at[above_z, 2:4, 0, :, own_lanes], 5, near_z(3))
    forward(2)
    forward(3)
    pl.loop(0, 2)(read_local)

    z_copies = []
    for group, (low, high) in enumerate(GROUPS):
        hear(ring_x, x_recv, group, low, high, x, lambda origin: z * 4 + origin)
        ring_z[z, :, low:high] = mixed(ring_x, 8, low, high).astype(BF16)
        for number, step in enumerate((2, 1, 3)):
            z_copies.append(
                copy(
                    ring_z.at[z, :, low:high],
                    ring_z.at[z, :, low:high],
                    z_send.at[group, number],
                    z_recv.at[group, number],
                    (near_z(step), head),
                )
            )
            z_copies[-1].start()
        buckets[0, :, low:high] = split(mixed(ring_x, 0, low, high), 0)
        buckets[1, :, low:high] = split(mixed(ring_x, 4, low, high), 0)

    arrived(2)
    arrived(3)
    pass_on(all_weight.at[0:2, below_x, 1, :, own_lanes], 6, near_x(1))
    pass_on(all_weight.at[2:4, above_x, 1, :, own_lanes], 7, near_x(3))
    forward(4)
    forward(5)

    def read_levels(start, count, low):
        tokens = pl.ds(pl.multiple_of(start, CHUNK), count)
        reader = readers[tokens, :]
        expanded = dot(
            jnp.concatenate([factors[low, tokens, :], factors[low + 1, tokens, :]], axis=0),
            expander[...],
        )
        return expanded[:count] * dot(reader, buckets[0]) + expanded[count:] * dot(
            reader, buckets[1]
        )

    @pl.loop(0, 4)
    def _(pair):
        output[pair] = output[pair] + read_levels(pair * 256, 256, 5)

    for number in (4, 5, 6, 7):
        arrived(number)
        forward(number + 2)

    for group, (low, high) in enumerate(GROUPS):
        hear(ring_z, z_recv, group, low, high, z, lambda origin: origin * 4 + x)
        buckets[0, :, low:high] = split(mixed(ring_z, 12, low, high), 0)
        buckets[1, :, low:high] = split(mixed(ring_z, 16, low, high), 0)

    same_head = (
        iota((256, LANES), 0) % LANES // WIDTH == iota((256, LANES), 1) // WIDTH
    ).astype(F32).astype(BF16)

    gain_row = gain[...].reshape(1, FEATS)

    def finish(pair, side):
        here = pl.ds(pl.multiple_of(side * CHUNK, CHUNK), CHUNK)
        total = output[pair, here, :] + read_levels(pair * 256 + side * CHUNK, CHUNK, 7)
        pieces = []
        for group in range(FEATS // LANES):
            part = total[:, group * LANES : (group + 1) * LANES]
            mean_square = dot(split(part * part), same_head) * (1.0 / WIDTH)
            scaled = part * lax.rsqrt(mean_square + EPSILON)
            pieces.append(scaled * gain_row[:, group * LANES : (group + 1) * LANES])
        return jnp.concatenate(pieces, axis=1).astype(BF16)

    def place_chip(place):
        return lax.rem(y + (2, 1, 3, 0)[place], 4)

    normed_copies = []

    def hand_over(place):
        normed_send[place] = finish(place_chip(place), 1 - core)
        normed_copies.append(
            copy(
                normed_send.at[place],
                normed_all.at[place, :, own_lanes],
                n_send.at[place],
                n_recv.at[place],
                (ctx, partner),
            )
        )
        normed_copies[-1].start()

    def keep(place):
        normed_all[place, :, own_lanes] = finish(place_chip(place), core)

    hand_over(0)
    keep(0)
    hand_over(1)
    for number, slab in enumerate(slabs):
        copy(
            slab(other_lanes),
            slab(other_lanes),
            wf_send.at[number],
            wf_recv.at[number],
            (ctx, partner),
        ).wait_recv()

    up = (ctx, lax.rem(y + 1, 4) * 2 + core)
    down = (ctx, lax.rem(y + 3, 4) * 2 + core)
    partial_copies = []

    def product(first_place, last_place, quarter):
        count = last_place - first_place
        return dot(
            normed_all[first_place:last_place].reshape(count * CHUNK, 2 * FEATS),
            all_weight[quarter].reshape(TILE, 2 * FEATS),
            NT,
        )

    def send(value, place, quarter, target, send_sems, recv_sems, device):
        partial_send[place, quarter] = value.astype(BF16)
        item = copy(
            partial_send.at[place, quarter], target, send_sems, recv_sems, device
        )
        item.start()
        partial_copies.append(item)

    normed_copies[0].wait_recv()
    for quarter in (0, 2, 1, 3):
        send(
            product(0, 1, quarter),
            0,
            quarter,
            relay_recv.at[quarter],
            r_send.at[quarter],
            r_recv.at[quarter],
            up if quarter < 2 else down,
        )
    keep(1)
    hand_over(2)
    keep(2)
    normed_copies[1].wait_recv()
    normed_copies[2].wait_recv()

    def send_near(value, place, quarter):
        send(
            value,
            place,
            quarter,
            partial_recv.at[place - 1, quarter],
            p_send.at[place - 1, quarter],
            p_recv.at[place - 1, quarter],
            up if place == 1 else down,
        )

    for quarter in (2, 0, 3, 1):
        both = product(1, 3, quarter)
        if quarter < 2:
            held[quarter] = both[:CHUNK]
            send_near(both[CHUNK:], 2, quarter)
        else:
            send_near(both[:CHUNK], 1, quarter)
            held[quarter] = both[CHUNK:]
    hand_over(3)
    keep(3)
    for quarter in (0, 2, 1, 3):
        partial_copies[(0, 2, 1, 3).index(quarter)].wait_recv()
        send_near(
            held[quarter] + relay_recv[quarter].astype(F32),
            1 if quarter < 2 else 2,
            quarter,
        )
    normed_copies[3].wait_recv()
    for quarter in range(4):
        own_sum[:, quarter * TILE : (quarter + 1) * TILE] = product(3, 4, quarter)
    for quarter in range(4):
        for place in range(2):
            copy(
                partial_recv.at[place, quarter],
                partial_recv.at[place, quarter],
                p_send.at[place, quarter],
                p_recv.at[place, quarter],
                up,
            ).wait_recv()
        columns = slice(quarter * TILE, (quarter + 1) * TILE)
        result[:, columns] = (
            own_sum[:, columns]
            + partial_recv[0, quarter].astype(F32)
            + partial_recv[1, quarter].astype(F32)
        ).astype(BF16)

    for item in (
        value_copies
        + first_copies
        + total_copies
        + second_copies
        + forward_copies
        + x_copies
        + z_copies
        + normed_copies
        + partial_copies
    ):
        item.wait_send()


def on_device(
    values,
    state_in,
    state_out,
    log_decay,
    level_class,
    level_table,
    skip_gain,
    norm_gain,
    out_weight,
):
    columns = out_weight.shape[1]
    weight = out_weight.T.reshape(2, columns // 2, FEATS)
    anywhere = pl.BlockSpec(memory_space=pl.ANY)
    dma = pltpu.SemaphoreType.DMA
    groups = len(GROUPS)
    return pl.pallas_call(
        kernel,
        out_shape=jax.ShapeDtypeStruct((CHUNK, OUTS), BF16),
        in_specs=[anywhere] * 9,
        out_specs=pl.BlockSpec(memory_space=pltpu.VMEM),
        scratch_shapes=[
            pltpu.VMEM((4, 2 * CHUNK, FEATS), BF16),
            pltpu.VMEM((CHUNKS * CHUNK, STATE), BF16),
            pltpu.VMEM((CHUNKS * CHUNK, STATE), BF16),
            pltpu.VMEM((HEADS_DEV, CHUNKS * CHUNK), F32),
            pltpu.VMEM((CHUNKS, CHUNK), jnp.int32),
            pltpu.VMEM((9, HEADS_DEV, 32), F32),
            pltpu.VMEM((1, HEADS_DEV), F32),
            pltpu.VMEM((FEATS,), F32),
            pltpu.VMEM((4, 4, 2, 80, 2 * FEATS), BF16),
            pltpu.VMEM((256, FEATS), BF16),
            pltpu.VMEM((CHUNKS * CHUNK, LANES), F32),
            pltpu.VMEM((16, LANES), F32),
            pltpu.VMEM((10, CHUNKS * CHUNK, 2 * LANES), BF16),
            pltpu.VMEM((CHUNKS, 4 * CHUNK, 2 * STATE), BF16),
            pltpu.VMEM((CHUNKS * CHUNK, 2 * STATE), BF16),
            pltpu.VMEM((4, 4, 8, LANES), F32),
            pltpu.VMEM((32, FEATS), F32),
            pltpu.VMEM((32, FEATS), F32),
            pltpu.VMEM((4, STATE, FEATS), F32),
            pltpu.VMEM((4, STATE, FEATS), F32),
            pltpu.VMEM((2, STATE, FEATS), F32),
            pltpu.VMEM((4, 2 * CHUNK, FEATS), F32),
            pltpu.VMEM((4, STATE, FEATS), BF16),
            pltpu.VMEM((4, STATE, FEATS), BF16),
            pltpu.VMEM((2, 2 * STATE, FEATS), BF16),
            pltpu.VMEM((4, CHUNK, FEATS), BF16),
            pltpu.VMEM((4, CHUNK, 2 * FEATS), BF16),
            pltpu.VMEM((CHUNK, OUTS), F32),
            pltpu.VMEM((4, CHUNK, TILE), F32),
            pltpu.VMEM((3, 4, CHUNK, TILE), BF16),
            pltpu.VMEM((4, CHUNK, TILE), BF16),
            pltpu.VMEM((2, 4, CHUNK, TILE), BF16),
            dma((8,)),
            dma((groups, 8)),
            dma((groups, 8)),
            dma((6,)),
            dma((6,)),
            dma((8,)),
            dma((8,)),
            dma((10,)),
            dma((10,)),
            dma((8,)),
            dma((8,)),
            dma((groups, 3)),
            dma((groups, 3)),
            dma((groups, 3)),
            dma((groups, 3)),
            dma((4,)),
            dma((4,)),
            dma((4,)),
            dma((4,)),
            dma((2, 4)),
            dma((2, 4)),
        ],
        compiler_params=pltpu.CompilerParams(
            collective_id=0,
            has_side_effects=True,
            vmem_limit_bytes=60 * 1024 * 1024,
        ),
        name="layer",
    )(
        values,
        state_in,
        state_out,
        log_decay.T,
        level_class.reshape(CHUNKS, CHUNK),
        level_table.transpose(1, 2, 0),
        skip_gain.reshape(1, -1),
        norm_gain,
        weight,
    )


def solution(mesh):
    return jax.shard_map(
        on_device,
        mesh=mesh,
        in_specs=(
            P(("ctx", "head"), None),
            P("ctx", None),
            P("ctx", None),
            P("ctx", "head"),
            P("ctx"),
            P(None, None, "head"),
            P("head"),
            P("head"),
            P("head", "ctx"),
        ),
        out_specs=P(("ctx", "head"), None),
        check_vma=False,
    )
```
